768 devices in a mesh: sx: 192 (over z, y, core), sy: 4 (over x).
Axes of the slice: x: 4, y: 8, z: 12, core: 2. Of those that a mesh axis runs over, the one named last changes fastest.
Arguments:
- flexibility: bfloat16 [192, 4, 1536, 1536], P('sx', 'sy'), as said below
- loads: bfloat16 [192, 4, 36, 1536], P('sx', 'sy'), may hold values from -32 to 32
- face_sizes: int32 [192, 4, 2], replicated, may hold values from 96 to 384, as said below
- face_owner: int32 [192, 4, 2], replicated, may hold values from 0 to 1
Outputs:
- multipliers: bfloat16 [192, 4, 2, 36, 384], P('sx', 'sy')
The draws below stay inside these ranges and needn't reach their ends.
Inputs may be any that keep to these rules, and one draw needn't show every extreme that they name: `flexibility`: each matrix is symmetric positive definite. Slots 0 to face_sizes - 1 of a face are live; entries for the grid's last row (index 0) or last column (index 1) are unused; some face has 384 live slots. `face_owner`: 0: the subdomain with the lower index carries the plus sign.
All inputs are finite; a program needn't handle non-finite values.
Results may differ from the reference program's by a relative error of at most 0.0044.
Values may be sent and summed in bfloat16 or wider, within the bound.
A program may use at most 32 MiB of HBM per device.

```python
import math
import jax
import jax.numpy as jnp
from jax import lax

FACE = 384
NB = 1536
LOADS = 36
ITERS = 2
NGX = 192
NGY = 4


def draw_flexibility(key, part):
    sub_count = NGX * NGY
    half_range = 2.2 / math.sqrt(NB)
    level_log = math.log(4.0)

    def make_block(block_index):
        sub_key = jax.random.fold_in(key, block_index)
        row_place = (block_index // NGY).astype(jnp.float32) / float(NGX - 1)
        col_place = (block_index % NGY).astype(jnp.float32) / float(NGY - 1)
        grid_level = jnp.exp(level_log * (row_place + col_place))
        raw_block = jax.random.uniform(jax.random.fold_in(sub_key, 1), (NB, NB), jnp.float32, -half_range, half_range)
        diagonal = jax.random.uniform(jax.random.fold_in(sub_key, 2), (NB,), jnp.float32, 2.5, 5.0)
        matrix = 0.5 * (raw_block + raw_block.T) + jnp.eye(NB, dtype=jnp.float32) * diagonal[None, :]
        return (grid_level * matrix).astype(jnp.bfloat16)
    return lax.map(make_block, jnp.arange(sub_count, dtype=jnp.int32)).reshape(NGX, NGY, NB, NB)


def draw_loads(key, part):
    base = jnp.clip(jax.random.normal(jax.random.fold_in(key, 21), (NGX, NGY, LOADS, NB), jnp.float32), -4.0, 4.0)
    row_place = 2.0 * jnp.arange(NGX, dtype=jnp.float32) / float(NGX - 1) - 1.0
    col_place = 2.0 * jnp.arange(NGY, dtype=jnp.float32) / float(NGY - 1) - 1.0
    row_tilt = jax.random.uniform(jax.random.fold_in(key, 22), (LOADS,), jnp.float32, -1.2, 1.2)
    col_tilt = jax.random.uniform(jax.random.fold_in(key, 23), (LOADS,), jnp.float32, -0.4, 0.4)
    rough = jax.random.uniform(jax.random.fold_in(key, 24), (NGX, NGY, LOADS), jnp.float32, -0.3, 0.3)
    level = jnp.exp(row_place[:, None, None] * row_tilt[None, None, :] + col_place[None, :, None] * col_tilt[None, None, :] + rough)
    return (base * level[..., None]).astype(jnp.bfloat16)


def draw_face_sizes(key, part):
    drawn_sizes = jax.random.randint(jax.random.fold_in(key, 11), (NGX, NGY, 2), FACE // 4, FACE + 1)
    return drawn_sizes.at[0, 0, 0].set(FACE).astype(jnp.int32)


def plant(entries, rng, low, top_value):
    longest = entries.shape.index(max(entries.shape))
    spots = []
    for shift in (0, 1):
        where = [jax.random.randint(jax.random.fold_in(rng, axis), (), 0, length) for axis, length in enumerate(entries.shape)]
        where[longest] = (where[longest] + shift) % entries.shape[longest]
        spots.append(tuple(where))
    return entries.at[spots[0]].set(low).at[spots[1]].set(top_value)


def setup_inputs(seed: int = 0) -> dict:
    key_of = jax.random.split(jax.random.key(seed), 5)
    flexibility = draw_flexibility(jax.random.fold_in(key_of[4], 71), 0)
    loads = draw_loads(jax.random.fold_in(key_of[4], 71), 0)
    face_sizes = draw_face_sizes(jax.random.fold_in(key_of[4], 71), 0)
    face_owner = plant(jax.random.randint(key_of[3], (NGX, NGY, 2), 0, 2), jax.random.fold_in(key_of[3], 1), 0, 1).astype(jnp.int32)
    return dict(flexibility=flexibility, loads=loads, face_sizes=face_sizes, face_owner=face_owner)


def face_coefficients(face_sizes, face_owner, face_kind):
    positions = jnp.arange(FACE, dtype=jnp.int32)
    row_index = jnp.arange(NGX, dtype=jnp.int32)[:, None]
    col_index = jnp.arange(NGY, dtype=jnp.int32)[None, :]
    if face_kind == 0:
        inside = jnp.broadcast_to(row_index < NGX - 1, (NGX, NGY))
    else:
        inside = jnp.broadcast_to(col_index < NGY - 1, (NGX, NGY))
    live_mask = (positions[None, None, :] < face_sizes[:, :, face_kind][:, :, None]) & inside[:, :, None]
    owner_sign = (1 - 2 * face_owner[:, :, face_kind]).astype(jnp.float32)[:, :, None]
    return jnp.where(live_mask, owner_sign, jnp.float32(0.0))


def shift_low(values, direction):
    zero_rim = jnp.zeros_like(lax.slice_in_dim(values, 0, 1, axis=direction))
    kept = lax.slice_in_dim(values, 0, values.shape[direction] - 1, axis=direction)
    return jnp.concatenate([zero_rim, kept], axis=direction)


def shift_high(values, direction):
    zero_rim = jnp.zeros_like(lax.slice_in_dim(values, 0, 1, axis=direction))
    kept = lax.slice_in_dim(values, 1, values.shape[direction], axis=direction)
    return jnp.concatenate([kept, zero_rim], axis=direction)


def interface_load(coef_x, coef_y, part_x, part_y):
    sent_x = (coef_x[:, :, None, :] * part_x).astype(jnp.bfloat16)
    sent_y = (coef_y[:, :, None, :] * part_y).astype(jnp.bfloat16)
    return jnp.concatenate([-shift_low(sent_x, 0), sent_x, -shift_low(sent_y, 1), sent_y], axis=3)


def apply_flex(flexibility, pushed):
    flat_matrices = flexibility.reshape(NGX * NGY, NB, NB)
    flat_pushed = pushed.reshape(NGX * NGY, LOADS, NB)

    def product(operands):
        return jnp.dot(operands[1], operands[0], preferred_element_type=jnp.float32)

    return lax.map(product, (flat_matrices, flat_pushed)).reshape(NGX, NGY, LOADS, NB)


def face_jumps(coef_x, coef_y, images):
    jump_x = coef_x[:, :, None, :] * (images[..., FACE:2 * FACE] - shift_high(images[..., 0:FACE], 0))
    jump_y = coef_y[:, :, None, :] * (images[..., 3 * FACE:4 * FACE] - shift_high(images[..., 2 * FACE:3 * FACE], 1))
    return jump_x, jump_y


def face_total(first_factor, second_factor):
    return jnp.sum(first_factor, axis=(0, 1, 3)) + jnp.sum(second_factor, axis=(0, 1, 3))


def per_load(values):
    return values[None, None, :, None]


def reference(flexibility, loads, face_sizes, face_owner):
    coef_x = face_coefficients(face_sizes, face_owner, 0)
    coef_y = face_coefficients(face_sizes, face_owner, 1)
    right_x, right_y = face_jumps(coef_x, coef_y, apply_flex(flexibility, loads))
    resid_x, resid_y = right_x, right_y
    search_x, search_y = right_x, right_y
    mult_x = jnp.zeros_like(right_x)
    mult_y = jnp.zeros_like(right_y)
    norm_now = face_total(resid_x * resid_x, resid_y * resid_y)
    for iteration in range(ITERS):
        pushed = interface_load(coef_x, coef_y, search_x, search_y)
        image_x, image_y = face_jumps(coef_x, coef_y, apply_flex(flexibility, pushed))
        step_size = per_load(norm_now / face_total(search_x * image_x, search_y * image_y))
        mult_x = mult_x + step_size * search_x
        mult_y = mult_y + step_size * search_y
        resid_x = resid_x - step_size * image_x
        resid_y = resid_y - step_size * image_y
        if iteration + 1 < ITERS:
            norm_next = face_total(resid_x * resid_x, resid_y * resid_y)
            momentum = per_load(norm_next / norm_now)
            search_x = resid_x + momentum * search_x
            search_y = resid_y + momentum * search_y
            norm_now = norm_next
    return jnp.stack([mult_x, mult_y], axis=2).astype(jnp.bfloat16)
```

```python
import functools

import jax
import jax.numpy as jnp
from jax import lax
from jax.experimental import pallas as pl
from jax.experimental.pallas import tpu as pltpu
from jax.sharding import PartitionSpec as P

FACE = 384
NB = 4 * FACE
HALF = 2 * FACE
LOADS = 36
NX, NY, NZ = 4, 8, 12
NSX = NZ * NY * 2
MESH = pl.DeviceIdType.MESH
F32 = jnp.float32
BF16 = jnp.bfloat16
ROWS = (1, 3, 0, 2)
COLS = (0, 2, 1, 3)


class Place:
    def __init__(self):
        self.sx = lax.axis_index("sx")
        self.sy = lax.axis_index("sy")
        self.core = lax.rem(self.sx, 2)
        self.y = lax.rem(self.sx // 2, NY)
        self.z = self.sx // (2 * NY)
        self.near = self.sy * 2 + self.core

    def down(self):
        return (lax.rem(self.sx + 1, NSX), self.sy)

    def up(self):
        return (lax.rem(self.sx + NSX - 1, NSX), self.sy)

    def right(self):
        return (self.sx, lax.rem(self.sy + 1, NX))

    def left(self):
        return (self.sx, lax.rem(self.sy + NX - 1, NX))

    def stage(self, which, k):
        if which == 0:
            slot = lax.rem(self.near + k, 2 * NX)
            return (self.sx - self.core + lax.rem(slot, 2), slot // 2)
        if which == 1:
            y = lax.rem(self.y + k, NY)
            return ((self.z * NY + y) * 2 + self.core, self.sy)
        z = lax.rem(self.z + k, NZ)
        return ((z * NY + self.y) * 2 + self.core, self.sy)

    def slot(self, which):
        return (self.near, self.y, self.z)[which]


STAGES = (2 * NX, NY, NZ)


def greet(place):
    barrier = pltpu.get_barrier_semaphore()
    peers = [place.down(), place.up()]
    for which, size in enumerate(STAGES):
        peers += [place.stage(which, k) for k in range(1, size)]
    for peer in peers:
        pl.semaphore_signal(barrier, inc=1, device_id=peer, device_id_type=MESH)
    return functools.partial(pl.semaphore_wait, barrier, len(peers))


def remote(src, dst, send_sem, recv_sem, peer):
    return pltpu.make_async_remote_copy(
        src_ref=src, dst_ref=dst, send_sem=send_sem, recv_sem=recv_sem, device_id=peer, device_id_type=MESH
    )


def diagonal(offset):
    row = lax.broadcasted_iota(jnp.int32, (LOADS, 128), 0)
    lane = lax.broadcasted_iota(jnp.int32, (LOADS, 128), 1)
    return lane == row + offset


def lanes(product, offset):
    column = jnp.sum(product, axis=1, keepdims=True)
    return jnp.sum(jnp.where(diagonal(offset), column, 0.0), axis=0, keepdims=True)


def column(row, offset):
    return jnp.sum(jnp.where(diagonal(offset), row, 0.0), axis=1, keepdims=True)


class Sums:
    def __init__(self, place, bufs, send_sems, recv_sems):
        self.place, self.bufs, self.send_sems, self.recv_sems = place, bufs, send_sems, recv_sems
        self.sent = []

    def __call__(self, index, value):
        for which, size in enumerate(STAGES):
            buf = self.bufs[which].at[index]
            mine = self.place.slot(which)
            buf[mine] = value
            copies = []
            for k in range(1, size):
                copies.append(
                    remote(
                        buf.at[mine],
                        buf.at[mine],
                        self.send_sems[which].at[index, k],
                        self.recv_sems[which].at[index, k],
                        self.place.stage(which, k),
                    )
                )
                copies[-1].start()
            for copy in copies:
                copy.wait_recv()
            value = buf[0]
            for k in range(1, size):
                value = value + buf[k]
            self.sent += copies
        return value


def exact_kernel(
    flex_hbm, loads_hbm, sizes_hbm, owner_hbm, out_ref,
    flex, loads, meta, z_out, z_in, u_out, u_in, acc, vec,
    buf0, buf1, buf2,
    load_sem, z_sem, u_sem, send0, send1, send2, recv0, recv1, recv2,
):
    place = Place()
    wait_all_in = greet(place)
    reads = start_reads(place, flex_hbm, loads_hbm, sizes_hbm, owner_hbm, flex, loads, meta, load_sem)
    total = Sums(place, (buf0, buf1, buf2), (send0, send1, send2), (recv0, recv1, recv2))
    sent = []

    for copy in reads["meta"] + reads["loads"]:
        copy.wait()
    cx, cy = coefficients(place, meta)

    def send_images(step):
        u_out[step, 0] = acc[:, 0:FACE]
        u_out[step, 1] = acc[:, FACE:HALF]
        copies = [
            remote(u_out.at[step, 0], u_in.at[step, 0], u_sem.at[0, step, 0], u_sem.at[1, step, 0], place.up()),
            remote(u_out.at[step, 1], u_in.at[step, 1], u_sem.at[0, step, 1], u_sem.at[1, step, 1], place.left()),
        ]
        for copy in copies:
            copy.start()
        sent.extend(copies)
        return copies

    def jumps(step, copies):
        for copy in copies:
            copy.wait_recv()
        jx = cx * (acc[:, HALF : HALF + FACE] - u_in[step, 0])
        jy = cy * (acc[:, HALF + FACE :] - u_in[step, 1])
        return jx, jy

    def operate(step, px, py):
        wx = (cx * px).astype(BF16)
        wy = (cy * py).astype(BF16)
        z_out[step, 0] = wx
        z_out[step, 1] = wy
        copies = [
            remote(z_out.at[step, 0], z_in.at[step, 0], z_sem.at[0, step, 0], z_sem.at[1, step, 0], place.down()),
            remote(z_out.at[step, 1], z_in.at[step, 1], z_sem.at[0, step, 1], z_sem.at[1, step, 1], place.right()),
        ]
        for copy in copies:
            copy.start()
        sent.extend(copies)
        own = jnp.concatenate([wx, wy], axis=1)
        acc[...] = jnp.dot(own, flex[0:HALF, :], preferred_element_type=F32)
        for copy in copies:
            copy.wait_recv()
        got = jnp.concatenate([-z_in[step, 0], -z_in[step, 1]], axis=1)
        acc[:, 0:HALF] += jnp.dot(got, flex[HALF:, 0:HALF], preferred_element_type=F32)
        copies = send_images(step + 1)
        acc[:, HALF:] += jnp.dot(got, flex[HALF:, HALF:], preferred_element_type=F32)
        return jumps(step + 1, copies)

    for copy in reads["low"]:
        copy.wait()
    acc[:, 0:HALF] = jnp.dot(loads[...], flex[:, 0:HALF], preferred_element_type=F32)
    wait_all_in()
    copies = send_images(0)
    for copy in reads["high"]:
        copy.wait()
    acc[:, HALF:] = jnp.dot(loads[...], flex[:, HALF:], preferred_element_type=F32)
    px, py = jumps(0, copies)
    vec[0, 0] = px
    vec[0, 1] = py
    qx, qy = operate(0, px, py)
    px, py = vec[0, 0], vec[0, 1]
    both = total(0, lanes(px * px + py * py, 0) + lanes(px * qx + py * qy, 64))
    rr = column(both, 0)
    step0 = rr / column(both, 64)
    rx = px - step0 * qx
    ry = py - step0 * qy
    vec[1, 0] = step0 * px
    vec[1, 1] = step0 * py
    s = column(total(1, lanes(rx * rx + ry * ry, 0)), 0)
    px = rx + (s / rr) * px
    py = ry + (s / rr) * py
    vec[0, 0] = px
    vec[0, 1] = py
    qx, qy = operate(1, px, py)
    px, py = vec[0, 0], vec[0, 1]
    step1 = s / column(total(2, lanes(px * qx + py * qy, 0)), 0)
    out_ref[0] = (vec[1, 0] + step1 * px).astype(BF16)
    out_ref[1] = (vec[1, 1] + step1 * py).astype(BF16)
    for copy in sent + total.sent:
        copy.wait_send()


def start_reads(place, flex_hbm, loads_hbm, sizes_hbm, owner_hbm, flex, loads, meta, sem):
    reads = {
        "meta": [
            pltpu.make_async_copy(sizes_hbm.at[place.sy], meta.at[0], sem.at[0]),
            pltpu.make_async_copy(owner_hbm.at[place.sy], meta.at[1], sem.at[1]),
        ],
        "loads": [],
        "low": [],
        "high": [],
    }
    count = 2
    for at, block in enumerate(ROWS):
        reads["loads"].append(
            pltpu.make_async_copy(
                loads_hbm.at[0, 0, :, pl.ds(block * FACE, FACE)], loads.at[:, pl.ds(at * FACE, FACE)], sem.at[count]
            )
        )
        count += 1
    for col_at, col in enumerate(COLS):
        for at, block in enumerate(ROWS):
            reads["low" if col_at < 2 else "high"].append(
                pltpu.make_async_copy(
                    flex_hbm.at[0, 0, pl.ds(block * FACE, FACE), pl.ds(col * FACE, FACE)],
                    flex.at[pl.ds(at * FACE, FACE), pl.ds(col_at * FACE, FACE)],
                    sem.at[count],
                )
            )
            count += 1
    for group in ("loads", "low", "meta", "high"):
        for copy in reads[group]:
            copy.start()
    return reads


def coefficients(place, meta):
    lane = lax.broadcasted_iota(jnp.int32, (2, NSX), 1)
    here = lane == place.sx
    sizes = jnp.sum(jnp.where(here, meta[0].astype(F32), 0.0), axis=1, keepdims=True)
    owner = jnp.sum(jnp.where(here, meta[1].astype(F32), 0.0), axis=1, keepdims=True)
    spot = lax.broadcasted_iota(jnp.int32, (1, FACE), 1).astype(F32)
    sign = 1.0 - 2.0 * owner
    has_x = jnp.where(place.sx < NSX - 1, 1.0, 0.0).astype(F32)
    has_y = jnp.where(place.sy < NX - 1, 1.0, 0.0).astype(F32)
    cx = jnp.where(spot < sizes[0:1] * has_x, sign[0:1], 0.0)
    cy = jnp.where(spot < sizes[1:2] * has_y, sign[1:2], 0.0)
    return cx, cy


READS = 2 + 4 + 16


def exact(flexibility, loads, sizes, owner):
    return pl.pallas_call(
        exact_kernel,
        out_shape=jax.ShapeDtypeStruct((2, LOADS, FACE), BF16),
        in_specs=[pl.BlockSpec(memory_space=pl.ANY)] * 4,
        out_specs=pl.BlockSpec(memory_space=pltpu.VMEM),
        scratch_shapes=[
            pltpu.VMEM((NB, NB), BF16),
            pltpu.VMEM((LOADS, NB), BF16),
            pltpu.VMEM((2, 2, NSX), jnp.int32),
            pltpu.VMEM((2, 2, LOADS, FACE), BF16),
            pltpu.VMEM((2, 2, LOADS, FACE), BF16),
            pltpu.VMEM((3, 2, LOADS, FACE), F32),
            pltpu.VMEM((3, 2, LOADS, FACE), F32),
            pltpu.VMEM((LOADS, NB), F32),
            pltpu.VMEM((2, 2, LOADS, FACE), F32),
        ]
        + [pltpu.VMEM((3, size, 1, 128), F32) for size in STAGES]
        + [
            pltpu.SemaphoreType.DMA((READS,)),
            pltpu.SemaphoreType.DMA((2, 2, 2)),
            pltpu.SemaphoreType.DMA((2, 3, 2)),
        ]
        + [pltpu.SemaphoreType.DMA((3, size)) for size in STAGES] * 2,
        compiler_params=pltpu.CompilerParams(collective_id=0, has_side_effects=True),
        name="exact",
    )(flexibility, loads, sizes, owner)


def body(flexibility, loads, face_sizes, face_owner):
    sizes = jnp.transpose(face_sizes, (1, 2, 0))
    owner = jnp.transpose(face_owner, (1, 2, 0))
    return exact(flexibility, loads, sizes, owner)[None, None]


def solution(mesh):
    return jax.shard_map(
        body,
        mesh=mesh,
        in_specs=(P("sx", "sy", None, None), P("sx", "sy", None, None), P(), P()),
        out_specs=P("sx", "sy", None, None, None),
        check_vma=False,
    )
```

```python
import functools

import jax
import jax.numpy as jnp
from jax import lax
from jax.experimental import pallas as pl
from jax.experimental.pallas import tpu as pltpu
from jax.sharding import PartitionSpec as P

FACE = 384
NB = 4 * FACE
HALF = 2 * FACE
LOADS = 36
NX, NY, NZ = 4, 8, 12
NSX = NZ * NY * 2
MESH = pl.DeviceIdType.MESH
F32 = jnp.float32
BF16 = jnp.bfloat16
ROWS = (1, 3, 0, 2)
COLS = (0, 2, 1, 3)


class Place:
    def __init__(self):
        self.sx = lax.axis_index("sx")
        self.sy = lax.axis_index("sy")
        self.core = lax.rem(self.sx, 2)
        self.y = lax.rem(self.sx // 2, NY)
        self.z = self.sx // (2 * NY)
        self.near = self.sy * 2 + self.core

    def down(self):
        return (lax.rem(self.sx + 1, NSX), self.sy)

    def up(self):
        return (lax.rem(self.sx + NSX - 1, NSX), self.sy)

    def right(self):
        return (self.sx, lax.rem(self.sy + 1, NX))

    def left(self):
        return (self.sx, lax.rem(self.sy + NX - 1, NX))

    def stage(self, which, k):
        if which == 0:
            slot = lax.rem(self.near + k, 2 * NX)
            return (self.sx - self.core + lax.rem(slot, 2), slot // 2)
        if which == 1:
            y = lax.rem(self.y + k, NY)
            return ((self.z * NY + y) * 2 + self.core, self.sy)
        z = lax.rem(self.z + k, NZ)
        return ((z * NY + self.y) * 2 + self.core, self.sy)

    def slot(self, which):
        return (self.near, self.y, self.z)[which]


STAGES = (2 * NX, NY, NZ)


def greet(place):
    barrier = pltpu.get_barrier_semaphore()
    peers = [place.down(), place.up()]
    for which, size in enumerate(STAGES):
        peers += [place.stage(which, k) for k in range(1, size)]
    for peer in peers:
        pl.semaphore_signal(barrier, inc=1, device_id=peer, device_id_type=MESH)
    return functools.partial(pl.semaphore_wait, barrier, len(peers))


def remote(src, dst, send_sem, recv_sem, peer):
    return pltpu.make_async_remote_copy(
        src_ref=src, dst_ref=dst, send_sem=send_sem, recv_sem=recv_sem, device_id=peer, device_id_type=MESH
    )


def diagonal(offset):
    row = lax.broadcasted_iota(jnp.int32, (LOADS, 128), 0)
    lane = lax.broadcasted_iota(jnp.int32, (LOADS, 128), 1)
    return lane == row + offset


def lanes(product, offset):
    column = jnp.sum(product, axis=1, keepdims=True)
    return jnp.sum(jnp.where(diagonal(offset), column, 0.0), axis=0, keepdims=True)


def column(row, offset):
    return jnp.sum(jnp.where(diagonal(offset), row, 0.0), axis=1, keepdims=True)


class Sums:
    def __init__(self, place, bufs, send_sems, recv_sems):
        self.place, self.bufs, self.send_sems, self.recv_sems = place, bufs, send_sems, recv_sems
        self.sent = []

    def __call__(self, index, value):
        for which, size in enumerate(STAGES):
            buf = self.bufs[which].at[index]
            mine = self.place.slot(which)
            buf[mine] = value
            copies = []
            for k in range(1, size):
                copies.append(
                    remote(
                        buf.at[mine],
                        buf.at[mine],
                        self.send_sems[which].at[index, k],
                        self.recv_sems[which].at[index, k],
                        self.place.stage(which, k),
                    )
                )
                copies[-1].start()
            for copy in copies:
                copy.wait_recv()
            value = buf[0]
            for k in range(1, size):
                value = value + buf[k]
            self.sent += copies
        return value


def exact_kernel(
    flex_hbm, loads_hbm, sizes_hbm, owner_hbm, out_ref,
    flex, loads, meta, z_out, z_in, u_out, u_in, acc, vec,
    buf0, buf1, buf2,
    load_sem, z_sem, u_sem, send0, send1, send2, recv0, recv1, recv2,
):
    place = Place()
    wait_all_in = greet(place)
    reads = start_reads(place, flex_hbm, loads_hbm, sizes_hbm, owner_hbm, flex, loads, meta, load_sem)
    total = Sums(place, (buf0, buf1, buf2), (send0, send1, send2), (recv0, recv1, recv2))
    sent = []

    for copy in reads["meta"] + reads["loads"]:
        copy.wait()
    cx, cy = coefficients(place, meta)

    def send_images(step):
        u_out[step, 0] = acc[:, 0:FACE]
        u_out[step, 1] = acc[:, FACE:HALF]
        copies = [
            remote(u_out.at[step, 0], u_in.at[step, 0], u_sem.at[0, step, 0], u_sem.at[1, step, 0], place.up()),
            remote(u_out.at[step, 1], u_in.at[step, 1], u_sem.at[0, step, 1], u_sem.at[1, step, 1], place.left()),
        ]
        for copy in copies:
            copy.start()
        sent.extend(copies)
        return copies

    def jumps(step, copies):
        for copy in copies:
            copy.wait_recv()
        jx = cx * (acc[:, HALF : HALF + FACE] - u_in[step, 0])
        jy = cy * (acc[:, HALF + FACE :] - u_in[step, 1])
        return jx, jy

    def operate(step, px, py):
        wx = (cx * px).astype(BF16)
        wy = (cy * py).astype(BF16)
        z_out[step, 0] = wx
        z_out[step, 1] = wy
        copies = [
            remote(z_out.at[step, 0], z_in.at[step, 0], z_sem.at[0, step, 0], z_sem.at[1, step, 0], place.down()),
            remote(z_out.at[step, 1], z_in.at[step, 1], z_sem.at[0, step, 1], z_sem.at[1, step, 1], place.right()),
        ]
        for copy in copies:
            copy.start()
        sent.extend(copies)
        own = jnp.concatenate([wx, wy], axis=1)
        acc[...] = jnp.dot(own, flex[0:HALF, :], preferred_element_type=F32)
        for copy in copies:
            copy.wait_recv()
        got = jnp.concatenate([-z_in[step, 0], -z_in[step, 1]], axis=1)
        acc[:, 0:HALF] += jnp.dot(got, flex[HALF:, 0:HALF], preferred_element_type=F32)
        copies = send_images(step + 1)
        acc[:, HALF:] += jnp.dot(got, flex[HALF:, HALF:], preferred_element_type=F32)
        return jumps(step + 1, copies)

    for copy in reads["low"]:
        copy.wait()
    acc[:, 0:HALF] = jnp.dot(loads[...], flex[:, 0:HALF], preferred_element_type=F32)
    wait_all_in()
    copies = send_images(0)
    for copy in reads["high"]:
        copy.wait()
    acc[:, HALF:] = jnp.dot(loads[...], flex[:, HALF:], preferred_element_type=F32)
    px, py = jumps(0, copies)
    vec[0, 0] = px
    vec[0, 1] = py
    qx, qy = operate(0, px, py)
    px, py = vec[0, 0], vec[0, 1]
    both = total(0, lanes(px * px + py * py, 0) + lanes(px * qx + py * qy, 64))
    rr = column(both, 0)
    step0 = rr / column(both, 64)
    rx = px - step0 * qx
    ry = py - step0 * qy
    vec[1, 0] = step0 * px
    vec[1, 1] = step0 * py
    s = column(total(1, lanes(rx * rx + ry * ry, 0)), 0)
    px = rx + (s / rr) * px
    py = ry + (s / rr) * py
    vec[0, 0] = px
    vec[0, 1] = py
    qx, qy = operate(1, px, py)
    px, py = vec[0, 0], vec[0, 1]
    step1 = s / column(total(2, lanes(px * qx + py * qy, 0)), 0)
    out_ref[0] = (vec[1, 0] + step1 * px).astype(BF16)
    out_ref[1] = (vec[1, 1] + step1 * py).astype(BF16)
    for copy in sent + total.sent:
        copy.wait_send()


def start_reads(place, flex_hbm, loads_hbm, sizes_hbm, owner_hbm, flex, loads, meta, sem):
    reads = {
        "meta": [
            pltpu.make_async_copy(sizes_hbm.at[place.sy], meta.at[0], sem.at[0]),
            pltpu.make_async_copy(owner_hbm.at[place.sy], meta.at[1], sem.at[1]),
        ],
        "loads": [],
        "low": [],
        "high": [],
    }
    count = 2
    for at, block in enumerate(ROWS):
        reads["loads"].append(
            pltpu.make_async_copy(
                loads_hbm.at[0, 0, :, pl.ds(block * FACE, FACE)], loads.at[:, pl.ds(at * FACE, FACE)], sem.at[count]
            )
        )
        count += 1
    for col_at, col in enumerate(COLS):
        for at, block in enumerate(ROWS):
            reads["low" if col_at < 2 else "high"].append(
                pltpu.make_async_copy(
                    flex_hbm.at[0, 0, pl.ds(block * FACE, FACE), pl.ds(col * FACE, FACE)],
                    flex.at[pl.ds(at * FACE, FACE), pl.ds(col_at * FACE, FACE)],
                    sem.at[count],
                )
            )
            count += 1
    for group in ("loads", "low", "meta", "high"):
        for copy in reads[group]:
            copy.start()
    return reads


def coefficients(place, meta):
    lane = lax.broadcasted_iota(jnp.int32, (2, NSX), 1)
    here = lane == place.sx
    sizes = jnp.sum(jnp.where(here, meta[0].astype(F32), 0.0), axis=1, keepdims=True)
    owner = jnp.sum(jnp.where(here, meta[1].astype(F32), 0.0), axis=1, keepdims=True)
    spot = lax.broadcasted_iota(jnp.int32, (1, FACE), 1).astype(F32)
    sign = 1.0 - 2.0 * owner
    has_x = jnp.where(place.sx < NSX - 1, 1.0, 0.0).astype(F32)
    has_y = jnp.where(place.sy < NX - 1, 1.0, 0.0).astype(F32)
    cx = jnp.where(spot < sizes[0:1] * has_x, sign[0:1], 0.0)
    cy = jnp.where(spot < sizes[1:2] * has_y, sign[1:2], 0.0)
    return cx, cy


READS = 2 + 4 + 16


def exact(flexibility, loads, sizes, owner):
    return pl.pallas_call(
        exact_kernel,
        out_shape=jax.ShapeDtypeStruct((2, LOADS, FACE), BF16),
        in_specs=[pl.BlockSpec(memory_space=pl.ANY)] * 4,
        out_specs=pl.BlockSpec(memory_space=pltpu.VMEM),
        scratch_shapes=[
            pltpu.VMEM((NB, NB), BF16),
            pltpu.VMEM((LOADS, NB), BF16),
            pltpu.VMEM((2, 2, NSX), jnp.int32),
            pltpu.VMEM((2, 2, LOADS, FACE), BF16),
            pltpu.VMEM((2, 2, LOADS, FACE), BF16),
            pltpu.VMEM((3, 2, LOADS, FACE), F32),
            pltpu.VMEM((3, 2, LOADS, FACE), F32),
            pltpu.VMEM((LOADS, NB), F32),
            pltpu.VMEM((2, 2, LOADS, FACE), F32),
        ]
        + [pltpu.VMEM((3, size, 1, 128), F32) for size in STAGES]
        + [
            pltpu.SemaphoreType.DMA((READS,)),
            pltpu.SemaphoreType.DMA((2, 2, 2)),
            pltpu.SemaphoreType.DMA((2, 3, 2)),
        ]
        + [pltpu.SemaphoreType.DMA((3, size)) for size in STAGES] * 2,
        compiler_params=pltpu.CompilerParams(collective_id=0, has_side_effects=True),
        name="exact",
    )(flexibility, loads, sizes, owner)


def fast_kernel(
    flex_hbm, loads_hbm, sizes_hbm, owner_hbm, out_ref, good_ref,
    flex, loads, meta, z_out, z_in, d_out, d_in, q_out, q_in, acc, vec,
    buf0, buf1, buf2,
    load_sem, z_sem, u_sem, send0, send1, send2, recv0, recv1, recv2,
):
    place = Place()
    wait_all_in = greet(place)
    reads = start_reads(place, flex_hbm, loads_hbm, sizes_hbm, owner_hbm, flex, loads, meta, load_sem)
    total = Sums(place, (buf0, buf1, buf2), (send0, send1, send2), (recv0, recv1, recv2))
    sent = []

    for copy in reads["meta"] + reads["loads"]:
        copy.wait()
    cx, cy = coefficients(place, meta)

    def send_images(step, out, into):
        out[0] = acc[:, 0:FACE].astype(out.dtype)
        out[1] = acc[:, FACE:HALF].astype(out.dtype)
        copies = [
            remote(out.at[0], into.at[0], u_sem.at[0, step, 0], u_sem.at[1, step, 0], place.up()),
            remote(out.at[1], into.at[1], u_sem.at[0, step, 1], u_sem.at[1, step, 1], place.left()),
        ]
        for copy in copies:
            copy.start()
        sent.extend(copies)
        return copies

    def jumps(copies, into):
        for copy in copies:
            copy.wait_recv()
        jx = cx * (acc[:, HALF : HALF + FACE] - into[0].astype(F32))
        jy = cy * (acc[:, HALF + FACE :] - into[1].astype(F32))
        return jx, jy

    def send_search(step, vx, vy):
        wx = (cx * vx).astype(BF16)
        wy = (cy * vy).astype(BF16)
        z_out[step, 0] = wx
        z_out[step, 1] = wy
        copies = [
            remote(z_out.at[step, 0], z_in.at[step, 0], z_sem.at[0, step, 0], z_sem.at[1, step, 0], place.down()),
            remote(z_out.at[step, 1], z_in.at[step, 1], z_sem.at[0, step, 1], z_sem.at[1, step, 1], place.right()),
        ]
        for copy in copies:
            copy.start()
        sent.extend(copies)
        own = jnp.concatenate([wx, wy], axis=1)
        acc[...] = jnp.dot(own, flex[0:HALF, :], preferred_element_type=F32)
        return own, copies

    for copy in reads["low"]:
        copy.wait()
    acc[:, 0:HALF] = jnp.dot(loads[...], flex[:, 0:HALF], preferred_element_type=F32)
    wait_all_in()
    copies = send_images(0, d_out, d_in)
    for copy in reads["high"]:
        copy.wait()
    acc[:, HALF:] = jnp.dot(loads[...], flex[:, HALF:], preferred_element_type=F32)
    dx, dy = jumps(copies, d_in)
    own, copies = send_search(0, dx, dy)
    vec[0, 0] = dx
    vec[0, 1] = dy
    for copy in copies:
        copy.wait_recv()
    got = jnp.concatenate([-z_in[0, 0], -z_in[0, 1]], axis=1)
    acc[:, 0:HALF] += jnp.dot(got, flex[HALF:, 0:HALF], preferred_element_type=F32)
    copies = send_images(1, q_out, q_in)
    acc[:, HALF:] += jnp.dot(got, flex[HALF:, HALF:], preferred_element_type=F32)
    qx, qy = jumps(copies, q_in)
    own, copies = send_search(1, qx, qy)
    vec[1, 0] = qx
    vec[1, 1] = qy
    dx, dy = vec[0, 0], vec[0, 1]
    top = lanes(dx * dx + dy * dy, 0) + lanes(dx * qx + dy * qy, 64)
    bottom = lanes(qx * qx + qy * qy, 0)
    kept = own.astype(F32) * acc[:, HALF:]
    for copy in copies:
        copy.wait_recv()
    got = jnp.concatenate([z_in[1, 0], z_in[1, 1]], axis=1)
    crossed = jnp.dot(got, flex[HALF:, 0:HALF], preferred_element_type=F32) - 2.0 * acc[:, 0:HALF]
    bottom = bottom + lanes(kept + got.astype(F32) * crossed, 64)
    sums = total(0, jnp.concatenate([top, bottom], axis=0))
    dd, dq = column(sums[0:1], 0), column(sums[0:1], 64)
    qq, qw = column(sums[1:2], 0), column(sums[1:2], 64)
    a = dd / dq
    far = a * a * qq
    s = far - dd
    g = far / dd
    weight = a * a * qw
    curve = g * g * dq - 2.0 * a * g * qq + weight
    a1 = s / curve
    alpha = a + a1 * g
    beta = -a1 * a
    out_ref[0] = (alpha * vec[0, 0] + beta * vec[1, 0]).astype(BF16)
    out_ref[1] = (alpha * vec[0, 1] + beta * vec[1, 1]).astype(BF16)
    good = (s >= CLOSE * dd) & (curve >= CLOSE * weight) & (s < TOP) & (curve < TOP)
    for value in (dd, dq, qq, qw):
        good = good & (value > 1.0 / TOP) & (value < TOP)
    good_ref[0] = jnp.min(jnp.where(good, 1.0, 0.0)).astype(jnp.int32)
    for copy in sent + total.sent:
        copy.wait_send()


CLOSE = 2.0**-6
TOP = 1e30


def fast(flexibility, loads, sizes, owner):
    return pl.pallas_call(
        fast_kernel,
        out_shape=(jax.ShapeDtypeStruct((2, LOADS, FACE), BF16), jax.ShapeDtypeStruct((1,), jnp.int32)),
        in_specs=[pl.BlockSpec(memory_space=pl.ANY)] * 4,
        out_specs=(pl.BlockSpec(memory_space=pltpu.VMEM), pl.BlockSpec(memory_space=pltpu.SMEM)),
        scratch_shapes=[
            pltpu.VMEM((NB, NB), BF16),
            pltpu.VMEM((LOADS, NB), BF16),
            pltpu.VMEM((2, 2, NSX), jnp.int32),
            pltpu.VMEM((2, 2, LOADS, FACE), BF16),
            pltpu.VMEM((2, 2, LOADS, FACE), BF16),
            pltpu.VMEM((2, LOADS, FACE), F32),
            pltpu.VMEM((2, LOADS, FACE), F32),
            pltpu.VMEM((2, LOADS, FACE), BF16),
            pltpu.VMEM((2, LOADS, FACE), BF16),
            pltpu.VMEM((LOADS, NB), F32),
            pltpu.VMEM((2, 2, LOADS, FACE), F32),
        ]
        + [pltpu.VMEM((1, size, 2, 128), F32) for size in STAGES]
        + [
            pltpu.SemaphoreType.DMA((READS,)),
            pltpu.SemaphoreType.DMA((2, 2, 2)),
            pltpu.SemaphoreType.DMA((2, 2, 2)),
        ]
        + [pltpu.SemaphoreType.DMA((1, size)) for size in STAGES] * 2,
        compiler_params=pltpu.CompilerParams(collective_id=1, has_side_effects=True),
        name="fast",
    )(flexibility, loads, sizes, owner)


def body(flexibility, loads, face_sizes, face_owner):
    sizes = jnp.transpose(face_sizes, (1, 2, 0))
    owner = jnp.transpose(face_owner, (1, 2, 0))
    args = (flexibility, loads, sizes, owner)
    result, good = fast(*args)
    result = lax.cond(good[0] > 0, lambda: result, lambda: exact(*args))
    return result[None, None]

def solution(mesh):
    return jax.shard_map(
        body,
        mesh=mesh,
        in_specs=(P("sx", "sy", None, None), P("sx", "sy", None, None), P(), P()),
        out_specs=P("sx", "sy", None, None, None),
        check_vma=False,
    )
```

```python
import functools

import jax
import jax.numpy as jnp
from jax import lax
from jax.experimental import pallas as pl
from jax.experimental.pallas import tpu as pltpu
from jax.sharding import PartitionSpec as P

FACE = 384
NB = 4 * FACE
HALF = 2 * FACE
LOADS = 36
NX, NY, NZ = 4, 8, 12
NSX = NZ * NY * 2
MESH = pl.DeviceIdType.MESH
F32 = jnp.float32
BF16 = jnp.bfloat16
ROWS = (1, 3, 0, 2)
COLS = (0, 2, 1, 3)


class Place:
    def __init__(self):
        self.sx = lax.axis_index("sx")
        self.sy = lax.axis_index("sy")
        self.core = lax.rem(self.sx, 2)
        self.y = lax.rem(self.sx // 2, NY)
        self.z = self.sx // (2 * NY)
        self.near = self.sy * 2 + self.core

    def down(self):
        return (lax.rem(self.sx + 1, NSX), self.sy)

    def up(self):
        return (lax.rem(self.sx + NSX - 1, NSX), self.sy)

    def right(self):
        return (self.sx, lax.rem(self.sy + 1, NX))

    def left(self):
        return (self.sx, lax.rem(self.sy + NX - 1, NX))

    def stage(self, which, k):
        if which == 0:
            slot = lax.rem(self.near + k, 2 * NX)
            return (self.sx - self.core + lax.rem(slot, 2), slot // 2)
        if which == 1:
            y = lax.rem(self.y + k, NY)
            return ((self.z * NY + y) * 2 + self.core, self.sy)
        z = lax.rem(self.z + k, NZ)
        return ((z * NY + self.y) * 2 + self.core, self.sy)

    def slot(self, which):
        return (self.near, self.y, self.z)[which]


STAGES = (2 * NX, NY, NZ)


def greet(place):
    barrier = pltpu.get_barrier_semaphore()
    peers = [place.down(), place.up()]
    for which, size in enumerate(STAGES):
        peers += [place.stage(which, k) for k in range(1, size)]
    for peer in peers:
        pl.semaphore_signal(barrier, inc=1, device_id=peer, device_id_type=MESH)
    return functools.partial(pl.semaphore_wait, barrier, len(peers))


def remote(src, dst, send_sem, recv_sem, peer):
    return pltpu.make_async_remote_copy(
        src_ref=src, dst_ref=dst, send_sem=send_sem, recv_sem=recv_sem, device_id=peer, device_id_type=MESH
    )


def diagonal(offset):
    row = lax.broadcasted_iota(jnp.int32, (LOADS, 128), 0)
    lane = lax.broadcasted_iota(jnp.int32, (LOADS, 128), 1)
    return lane == row + offset


def lanes(product, offset):
    column = jnp.sum(product, axis=1, keepdims=True)
    return jnp.sum(jnp.where(diagonal(offset), column, 0.0), axis=0, keepdims=True)


def column(row, offset):
    return jnp.sum(jnp.where(diagonal(offset), row, 0.0), axis=1, keepdims=True)


class Sums:
    def __init__(self, place, bufs, send_sems, recv_sems):
        self.place, self.bufs, self.send_sems, self.recv_sems = place, bufs, send_sems, recv_sems
        self.sent = []

    def __call__(self, index, value):
        for which, size in enumerate(STAGES):
            buf = self.bufs[which].at[index]
            mine = self.place.slot(which)
            buf[mine] = value
            copies = []
            for k in range(1, size):
                copies.append(
                    remote(
                        buf.at[mine],
                        buf.at[mine],
                        self.send_sems[which].at[index, k],
                        self.recv_sems[which].at[index, k],
                        self.place.stage(which, k),
                    )
                )
                copies[-1].start()
            for copy in copies:
                copy.wait_recv()
            value = buf[0]
            for k in range(1, size):
                value = value + buf[k]
            self.sent += copies
        return value


def exact_kernel(
    flex_hbm, loads_hbm, sizes_hbm, owner_hbm, out_ref,
    flex, loads, meta, z_out, z_in, u_out, u_in, acc, vec,
    buf0, buf1, buf2,
    load_sem, z_sem, u_sem, send0, send1, send2, recv0, recv1, recv2,
):
    place = Place()
    wait_all_in = greet(place)
    reads = start_reads(place, flex_hbm, loads_hbm, sizes_hbm, owner_hbm, flex, loads, meta, load_sem)
    total = Sums(place, (buf0, buf1, buf2), (send0, send1, send2), (recv0, recv1, recv2))
    sent = []

    for copy in reads["meta"] + reads["loads"]:
        copy.wait()
    cx, cy = coefficients(place, meta)

    def send_images(step):
        u_out[step, 0] = acc[:, 0:FACE]
        u_out[step, 1] = acc[:, FACE:HALF]
        copies = [
            remote(u_out.at[step, 0], u_in.at[step, 0], u_sem.at[0, step, 0], u_sem.at[1, step, 0], place.up()),
            remote(u_out.at[step, 1], u_in.at[step, 1], u_sem.at[0, step, 1], u_sem.at[1, step, 1], place.left()),
        ]
        for copy in copies:
            copy.start()
        sent.extend(copies)
        return copies

    def jumps(step, copies):
        for copy in copies:
            copy.wait_recv()
        jx = cx * (acc[:, HALF : HALF + FACE] - u_in[step, 0])
        jy = cy * (acc[:, HALF + FACE :] - u_in[step, 1])
        return jx, jy

    def operate(step, px, py):
        wx = (cx * px).astype(BF16)
        wy = (cy * py).astype(BF16)
        z_out[step, 0] = wx
        z_out[step, 1] = wy
        copies = [
            remote(z_out.at[step, 0], z_in.at[step, 0], z_sem.at[0, step, 0], z_sem.at[1, step, 0], place.down()),
            remote(z_out.at[step, 1], z_in.at[step, 1], z_sem.at[0, step, 1], z_sem.at[1, step, 1], place.right()),
        ]
        for copy in copies:
            copy.start()
        sent.extend(copies)
        own = jnp.concatenate([wx, wy], axis=1)
        acc[...] = jnp.dot(own, flex[0:HALF, :], preferred_element_type=F32)
        for copy in copies:
            copy.wait_recv()
        got = jnp.concatenate([-z_in[step, 0], -z_in[step, 1]], axis=1)
        acc[:, 0:HALF] += jnp.dot(got, flex[HALF:, 0:HALF], preferred_element_type=F32)
        copies = send_images(step + 1)
        acc[:, HALF:] += jnp.dot(got, flex[HALF:, HALF:], preferred_element_type=F32)
        return jumps(step + 1, copies)

    for copy in reads["low"]:
        copy.wait()
    acc[:, 0:HALF] = jnp.dot(loads[...], flex[:, 0:HALF], preferred_element_type=F32)
    wait_all_in()
    copies = send_images(0)
    for copy in reads["high"]:
        copy.wait()
    acc[:, HALF:] = jnp.dot(loads[...], flex[:, HALF:], preferred_element_type=F32)
    px, py = jumps(0, copies)
    vec[0, 0] = px
    vec[0, 1] = py
    qx, qy = operate(0, px, py)
    px, py = vec[0, 0], vec[0, 1]
    both = total(0, lanes(px * px + py * py, 0) + lanes(px * qx + py * qy, 64))
    rr = column(both, 0)
    step0 = rr / column(both, 64)
    rx = px - step0 * qx
    ry = py - step0 * qy
    vec[1, 0] = step0 * px
    vec[1, 1] = step0 * py
    s = column(total(1, lanes(rx * rx + ry * ry, 0)), 0)
    px = rx + (s / rr) * px
    py = ry + (s / rr) * py
    vec[0, 0] = px
    vec[0, 1] = py
    qx, qy = operate(1, px, py)
    px, py = vec[0, 0], vec[0, 1]
    step1 = s / column(total(2, lanes(px * qx + py * qy, 0)), 0)
    out_ref[0] = (vec[1, 0] + step1 * px).astype(BF16)
    out_ref[1] = (vec[1, 1] + step1 * py).astype(BF16)
    for copy in sent + total.sent:
        copy.wait_send()


def start_reads(place, flex_hbm, loads_hbm, sizes_hbm, owner_hbm, flex, loads, meta, sem):
    reads = {
        "meta": [
            pltpu.make_async_copy(sizes_hbm.at[place.sy], meta.at[0], sem.at[0]),
            pltpu.make_async_copy(owner_hbm.at[place.sy], meta.at[1], sem.at[1]),
        ],
        "loads": [],
        "low": [],
        "high": [],
    }
    count = 2
    for at, block in enumerate(ROWS):
        reads["loads"].append(
            pltpu.make_async_copy(
                loads_hbm.at[0, 0, :, pl.ds(block * FACE, FACE)], loads.at[:, pl.ds(at * FACE, FACE)], sem.at[count]
            )
        )
        count += 1
    for col_at, col in enumerate(COLS):
        for at, block in enumerate(ROWS):
            reads["low" if col_at < 2 else "high"].append(
                pltpu.make_async_copy(
                    flex_hbm.at[0, 0, pl.ds(block * FACE, FACE), pl.ds(col * FACE, FACE)],
                    flex.at[pl.ds(at * FACE, FACE), pl.ds(col_at * FACE, FACE)],
                    sem.at[count],
                )
            )
            count += 1
    for group in ("loads", "low", "meta", "high"):
        for copy in reads[group]:
            copy.start()
    return reads


def coefficients(place, meta):
    lane = lax.broadcasted_iota(jnp.int32, (2, NSX), 1)
    here = lane == place.sx
    sizes = jnp.sum(jnp.where(here, meta[0].astype(F32), 0.0), axis=1, keepdims=True)
    owner = jnp.sum(jnp.where(here, meta[1].astype(F32), 0.0), axis=1, keepdims=True)
    spot = lax.broadcasted_iota(jnp.int32, (1, FACE), 1).astype(F32)
    sign = 1.0 - 2.0 * owner
    has_x = jnp.where(place.sx < NSX - 1, 1.0, 0.0).astype(F32)
    has_y = jnp.where(place.sy < NX - 1, 1.0, 0.0).astype(F32)
    cx = jnp.where(spot < sizes[0:1] * has_x, sign[0:1], 0.0)
    cy = jnp.where(spot < sizes[1:2] * has_y, sign[1:2], 0.0)
    return cx, cy


READS = 2 + 4 + 16


def exact(flexibility, loads, sizes, owner):
    return pl.pallas_call(
        exact_kernel,
        out_shape=jax.ShapeDtypeStruct((2, LOADS, FACE), BF16),
        in_specs=[pl.BlockSpec(memory_space=pl.ANY)] * 4,
        out_specs=pl.BlockSpec(memory_space=pltpu.VMEM),
        scratch_shapes=[
            pltpu.VMEM((NB, NB), BF16),
            pltpu.VMEM((LOADS, NB), BF16),
            pltpu.VMEM((2, 2, NSX), jnp.int32),
            pltpu.VMEM((2, 2, LOADS, FACE), BF16),
            pltpu.VMEM((2, 2, LOADS, FACE), BF16),
            pltpu.VMEM((3, 2, LOADS, FACE), F32),
            pltpu.VMEM((3, 2, LOADS, FACE), F32),
            pltpu.VMEM((LOADS, NB), F32),
            pltpu.VMEM((2, 2, LOADS, FACE), F32),
        ]
        + [pltpu.VMEM((3, size, 1, 128), F32) for size in STAGES]
        + [
            pltpu.SemaphoreType.DMA((READS,)),
            pltpu.SemaphoreType.DMA((2, 2, 2)),
            pltpu.SemaphoreType.DMA((2, 3, 2)),
        ]
        + [pltpu.SemaphoreType.DMA((3, size)) for size in STAGES] * 2,
        compiler_params=pltpu.CompilerParams(collective_id=0, has_side_effects=True),
        name="exact",
    )(flexibility, loads, sizes, owner)


def far(size, k):
    return min(k, size - k)


PLANE = sorted(((x, y) for x in range(NX) for y in range(NY) if x or y), key=lambda o: -far(NX, o[0]) - far(NY, o[1]))
LINE = sorted(((z, c) for z in range(NZ) for c in range(2) if z or c), key=lambda o: -2 * far(NZ, o[0]) - o[1])


class Partners:
    def __init__(self, place):
        self.slots = (place.sy * NY + place.y, place.z * 2 + place.core)
        plane = [
            ((place.z * NY + lax.rem(place.y + y, NY)) * 2 + place.core, lax.rem(place.sy + x, NX)) for x, y in PLANE
        ]
        line = [
            (
                (lax.rem(place.z + z, NZ) * NY + place.y) * 2 + (1 - place.core if c else place.core),
                place.sy,
            )
            for z, c in LINE
        ]
        self.stages = (plane, line)
        self.core = (place.sx + 1 - 2 * place.core, place.sy)

    @staticmethod
    def along_y(place, k):
        return ((place.z * NY + lax.rem(place.y + k + NY, NY)) * 2 + place.core, place.sy)

    @staticmethod
    def along_z(place, k):
        return ((lax.rem(place.z + k + NZ, NZ) * NY + place.y) * 2 + place.core, place.sy)


def fast_kernel(
    flex_hbm, loads_hbm, sizes_hbm, owner_hbm, out_ref, good_ref,
    flex, loads, meta, sign_meta, u0, r0, u1, r1, dvec, qvec,
    buf0, buf1,
    load_sem, u_sem, sum_sem, word,
):
    place = Place()
    left_sy = lax.rem(place.sy + NX - 1, NX)
    sem = iter(range(FAST_READS))
    load_read = pltpu.make_async_copy(loads_hbm.at[0, 0], loads, load_sem.at[next(sem)])
    flex_reads = {}
    for half in (1, 0):
        for block in range(4):
            spot = (pl.ds(block * FACE, FACE), pl.ds(half * HALF, HALF))
            flex_reads[half, block] = pltpu.make_async_copy(
                flex_hbm.at[(0, 0) + spot], flex.at[spot], load_sem.at[next(sem)]
            )
    meta_reads = [
        pltpu.make_async_copy(sizes_hbm.at[place.sy], meta.at[0], load_sem.at[next(sem)]),
        pltpu.make_async_copy(sizes_hbm.at[left_sy], meta.at[1], load_sem.at[next(sem)]),
        pltpu.make_async_copy(owner_hbm.at[place.sy], sign_meta, load_sem.at[next(sem)]),
    ]
    load_read.start()
    for half in (1, 0):
        for block in range(4):
            flex_reads[half, block].start()
    for copy in meta_reads:
        copy.start()
    partners = Partners(place)
    faces = (place.up(), place.down(), place.left(), place.right())
    near_y, near_z = [[along(place, k) for k in (1, -1)] for along in (partners.along_y, partners.along_z)]
    next_y, next_z = [[along(place, k) for k in (2, -2)] for along in (partners.along_y, partners.along_z)]
    rounds = (
        near_y + near_z,
        next_y + next_z,
        next_z + list(faces[2:]),
        [partners.core] + list(faces[2:]),
    )
    barrier = pltpu.get_barrier_semaphore()
    peers = list(faces) + near_y + near_z
    for peer in peers:
        pl.semaphore_signal(barrier, inc=1, device_id=peer, device_id_type=MESH)

    def tell(which):
        for peer in rounds[which]:
            pl.semaphore_signal(word.at[which], inc=1, device_id=peer, device_id_type=MESH)

    def hear(which):
        pl.semaphore_wait(word.at[which], len(rounds[which]))

    sent = []

    def exchange(step, half, source, into):
        copies = []
        for block in (2 * half, 2 * half + 1):
            copies.append(
                remote(
                    source.at[block], into.at[block ^ 1], u_sem.at[0, step, block], u_sem.at[1, step, block], faces[block]
                )
            )
            copies[-1].start()
        sent.extend(copies)
        return copies

    def product(rows, half, block):
        return jnp.dot(
            rows, flex[block * FACE : (block + 1) * FACE, half * HALF : (half + 1) * HALF], preferred_element_type=F32
        )

    def half_product(pair, row_half, col_half):
        return jnp.dot(
            pair,
            flex[row_half * HALF : (row_half + 1) * HALF, col_half * HALF : (col_half + 1) * HALF],
            preferred_element_type=F32,
        )

    load_read.wait()
    copies0 = {}
    for half in (1, 0):
        for block in range(2):
            flex_reads[half, block].wait()
        value = half_product(loads[:, 0:HALF], 0, half)
        for block in range(2, 4):
            flex_reads[half, block].wait()
        value = value + half_product(loads[:, HALF:], 1, half)
        u0[2 * half] = value[:, 0:FACE]
        u0[2 * half + 1] = value[:, FACE:]
        if half == 1:
            pl.semaphore_wait(barrier, len(peers))
        copies0[half] = exchange(0, half, u0, r0)
        if half == 1:
            tell(0)
    for copy in meta_reads:
        copy.wait()
    hear(0)
    tell(1)
    live, sign = live_faces(place, meta, sign_meta)
    hear(1)
    tell(2)

    def jump(half, copies, u, r, kept):
        for copy in copies[half]:
            copy.wait_recv()
        pair = []
        for block in (2 * half, 2 * half + 1):
            value = jnp.where(live[block], u[block] - r[block], 0.0)
            kept[block] = value
            pair.append(value.astype(BF16))
        return jnp.concatenate(pair, axis=1)

    pair = jump(0, copies0, u0, r0, dvec)
    low = [half_product(pair, 0, half) for half in range(2)]
    pair = jump(1, copies0, u0, r0, dvec)
    copies1 = {}
    for half in (1, 0):
        value = low[half] + half_product(pair, 1, half)
        u1[2 * half] = value[:, 0:FACE]
        u1[2 * half + 1] = value[:, FACE:]
        copies1[half] = exchange(1, half, u1, r1)
    hear(2)
    tell(3)
    top = lanes(dvec[1] * dvec[1] + dvec[3] * dvec[3], 0)
    first = jump(0, copies1, u1, r1, qvec)
    low = [half_product(first, 0, half) for half in range(2)]
    second = jump(1, copies1, u1, r1, qvec)
    inner = first.astype(F32) * low[0]
    inner = inner + second.astype(F32) * (2.0 * low[1] + half_product(second, 1, 1))
    top = top + lanes(dvec[1] * qvec[1] + dvec[3] * qvec[3], 64)
    bottom = lanes(qvec[1] * qvec[1] + qvec[3] * qvec[3], 0) + lanes(inner, 64)
    sums = jnp.concatenate([top, bottom], axis=0)
    hear(3)
    waits = []
    for which, (stage, mine, buf) in enumerate(zip(partners.stages, partners.slots, (buf0, buf1))):
        buf[mine] = sums
        for peer in stage:
            remote(buf.at[mine], buf.at[mine], sum_sem.at[0, which], sum_sem.at[1, which], peer).start()
        others = buf.at[pl.ds(0, len(stage))]
        waits.append(remote(others, others, sum_sem.at[0, which], sum_sem.at[1, which], stage[0]))
        waits[-1].wait_recv()
        terms = [buf[k] for k in range(len(stage) + 1)]
        while len(terms) > 1:
            terms = [sum(terms[k : k + 2]) for k in range(0, len(terms), 2)]
        sums = terms[0]
    dd, dq = column(sums[0:1], 0), column(sums[0:1], 64)
    qq, qw = column(sums[1:2], 0), column(sums[1:2], 64)
    a = dd / dq
    far = a * a * qq
    s = far - dd
    g = far / dd
    weight = a * a * qw
    curve = g * g * dq - 2.0 * a * g * qq + weight
    a1 = s / curve
    alpha = a + a1 * g
    beta = -a1 * a
    out_ref[0] = (sign[0] * (alpha * dvec[1] + beta * qvec[1])).astype(BF16)
    out_ref[1] = (sign[1] * (alpha * dvec[3] + beta * qvec[3])).astype(BF16)
    good = (s >= CLOSE * dd) & (curve >= CLOSE * weight) & (s < TOP) & (curve < TOP)
    for value in (dd, dq, qq, qw):
        good = good & (value > 1.0 / TOP) & (value < TOP)
    good_ref[0] = jnp.min(jnp.where(good, 1.0, 0.0)).astype(jnp.int32)
    for copy in sent + waits:
        copy.wait_send()


def live_faces(place, meta, sign_meta):
    lane = lax.broadcasted_iota(jnp.int32, (2, NSX), 1)

    def at(table, row):
        return jnp.sum(jnp.where(lane == row, table.astype(F32), 0.0), axis=1, keepdims=True)

    here = at(meta[0], place.sx)
    sizes = (
        at(meta[0], place.sx - 1)[0:1],
        here[0:1] * jnp.where(place.sx < NSX - 1, 1.0, 0.0).astype(F32),
        at(meta[1], place.sx)[1:2] * jnp.where(place.sy > 0, 1.0, 0.0).astype(F32),
        here[1:2] * jnp.where(place.sy < NX - 1, 1.0, 0.0).astype(F32),
    )
    spot = lax.broadcasted_iota(jnp.int32, (LOADS, FACE), 1).astype(F32)
    sign = 1.0 - 2.0 * at(sign_meta[...], place.sx)
    return [spot < size for size in sizes], (sign[0:1], sign[1:2])


FAST_READS = 1 + 8 + 3


CLOSE = 2.0**-6
TOP = 1e30


def fast(flexibility, loads, sizes, owner):
    def faces(dtype):
        return pltpu.VMEM((4, LOADS, FACE), dtype)

    return pl.pallas_call(
        fast_kernel,
        out_shape=(jax.ShapeDtypeStruct((2, LOADS, FACE), BF16), jax.ShapeDtypeStruct((1,), jnp.int32)),
        in_specs=[pl.BlockSpec(memory_space=pl.ANY)] * 4,
        out_specs=(pl.BlockSpec(memory_space=pltpu.VMEM), pl.BlockSpec(memory_space=pltpu.SMEM)),
        scratch_shapes=[
            pltpu.VMEM((NB, NB), BF16),
            pltpu.VMEM((LOADS, NB), BF16),
            pltpu.VMEM((2, 2, NSX), jnp.int32),
            pltpu.VMEM((2, NSX), jnp.int32),
            faces(F32),
            faces(F32),
            faces(F32),
            faces(F32),
            faces(F32),
            faces(F32),
        ]
        + [pltpu.VMEM((size, 2, 128), F32) for size in (NX * NY, 2 * NZ)]
        + [
            pltpu.SemaphoreType.DMA((FAST_READS,)),
            pltpu.SemaphoreType.DMA((2, 2, 4)),
            pltpu.SemaphoreType.DMA((2, 2)),
            pltpu.SemaphoreType.REGULAR((4,)),
        ],
        compiler_params=pltpu.CompilerParams(collective_id=1, has_side_effects=True),
        name="fast",
    )(flexibility, loads, sizes, owner)


def body(flexibility, loads, face_sizes, face_owner):
    sizes = jnp.transpose(face_sizes, (1, 2, 0))
    owner = jnp.transpose(face_owner, (1, 2, 0))
    args = (flexibility, loads, sizes, owner)
    result, good = fast(*args)
    result = lax.cond(good[0] > 0, lambda: result, lambda: exact(*args))
    return result[None, None]

def solution(mesh):
    return jax.shard_map(
        body,
        mesh=mesh,
        in_specs=(P("sx", "sy", None, None), P("sx", "sy", None, None), P(), P()),
        out_specs=P("sx", "sy", None, None, None),
        check_vma=False,
    )
```

```python
import functools

import jax
import jax.numpy as jnp
from jax import lax
from jax.experimental import pallas as pl
from jax.experimental.pallas import tpu as pltpu
from jax.sharding import PartitionSpec as P

FACE = 384
NB = 4 * FACE
HALF = 2 * FACE
LOADS = 36
NX, NY, NZ = 4, 8, 12
NSX = NZ * NY * 2
MESH = pl.DeviceIdType.MESH
F32 = jnp.float32
BF16 = jnp.bfloat16
ROWS = (1, 3, 0, 2)
COLS = (0, 2, 1, 3)


class Place:
    def __init__(self):
        self.sx = lax.axis_index("sx")
        self.sy = lax.axis_index("sy")
        self.core = lax.rem(self.sx, 2)
        self.y = lax.rem(self.sx // 2, NY)
        self.z = self.sx // (2 * NY)
        self.near = self.sy * 2 + self.core

    def down(self):
        return (lax.rem(self.sx + 1, NSX), self.sy)

    def up(self):
        return (lax.rem(self.sx + NSX - 1, NSX), self.sy)

    def right(self):
        return (self.sx, lax.rem(self.sy + 1, NX))

    def left(self):
        return (self.sx, lax.rem(self.sy + NX - 1, NX))

    def stage(self, which, k):
        if which == 0:
            slot = lax.rem(self.near + k, 2 * NX)
            return (self.sx - self.core + lax.rem(slot, 2), slot // 2)
        if which == 1:
            y = lax.rem(self.y + k, NY)
            return ((self.z * NY + y) * 2 + self.core, self.sy)
        z = lax.rem(self.z + k, NZ)
        return ((z * NY + self.y) * 2 + self.core, self.sy)

    def slot(self, which):
        return (self.near, self.y, self.z)[which]


STAGES = (2 * NX, NY, NZ)


def greet(place):
    barrier = pltpu.get_barrier_semaphore()
    peers = [place.down(), place.up()]
    for which, size in enumerate(STAGES):
        peers += [place.stage(which, k) for k in range(1, size)]
    for peer in peers:
        pl.semaphore_signal(barrier, inc=1, device_id=peer, device_id_type=MESH)
    return functools.partial(pl.semaphore_wait, barrier, len(peers))


def remote(src, dst, send_sem, recv_sem, peer):
    return pltpu.make_async_remote_copy(
        src_ref=src, dst_ref=dst, send_sem=send_sem, recv_sem=recv_sem, device_id=peer, device_id_type=MESH
    )


def diagonal(offset):
    row = lax.broadcasted_iota(jnp.int32, (LOADS, 128), 0)
    lane = lax.broadcasted_iota(jnp.int32, (LOADS, 128), 1)
    return lane == row + offset


def lanes(product, offset):
    column = jnp.sum(product, axis=1, keepdims=True)
    return jnp.sum(jnp.where(diagonal(offset), column, 0.0), axis=0, keepdims=True)


def column(row, offset):
    return jnp.sum(jnp.where(diagonal(offset), row, 0.0), axis=1, keepdims=True)


class Sums:
    def __init__(self, place, bufs, send_sems, recv_sems):
        self.place, self.bufs, self.send_sems, self.recv_sems = place, bufs, send_sems, recv_sems
        self.sent = []

    def __call__(self, index, value):
        for which, size in enumerate(STAGES):
            buf = self.bufs[which].at[index]
            mine = self.place.slot(which)
            buf[mine] = value
            copies = []
            for k in range(1, size):
                copies.append(
                    remote(
                        buf.at[mine],
                        buf.at[mine],
                        self.send_sems[which].at[index, k],
                        self.recv_sems[which].at[index, k],
                        self.place.stage(which, k),
                    )
                )
                copies[-1].start()
            for copy in copies:
                copy.wait_recv()
            value = buf[0]
            for k in range(1, size):
                value = value + buf[k]
            self.sent += copies
        return value


def exact_kernel(
    flex_hbm, loads_hbm, sizes_hbm, owner_hbm, out_ref,
    flex, loads, meta, z_out, z_in, u_out, u_in, acc, vec,
    buf0, buf1, buf2,
    load_sem, z_sem, u_sem, send0, send1, send2, recv0, recv1, recv2,
):
    place = Place()
    wait_all_in = greet(place)
    reads = start_reads(place, flex_hbm, loads_hbm, sizes_hbm, owner_hbm, flex, loads, meta, load_sem)
    total = Sums(place, (buf0, buf1, buf2), (send0, send1, send2), (recv0, recv1, recv2))
    sent = []

    for copy in reads["meta"] + reads["loads"]:
        copy.wait()
    cx, cy = coefficients(place, meta)

    def send_images(step):
        u_out[step, 0] = acc[:, 0:FACE]
        u_out[step, 1] = acc[:, FACE:HALF]
        copies = [
            remote(u_out.at[step, 0], u_in.at[step, 0], u_sem.at[0, step, 0], u_sem.at[1, step, 0], place.up()),
            remote(u_out.at[step, 1], u_in.at[step, 1], u_sem.at[0, step, 1], u_sem.at[1, step, 1], place.left()),
        ]
        for copy in copies:
            copy.start()
        sent.extend(copies)
        return copies

    def jumps(step, copies):
        for copy in copies:
            copy.wait_recv()
        jx = cx * (acc[:, HALF : HALF + FACE] - u_in[step, 0])
        jy = cy * (acc[:, HALF + FACE :] - u_in[step, 1])
        return jx, jy

    def operate(step, px, py):
        wx = (cx * px).astype(BF16)
        wy = (cy * py).astype(BF16)
        z_out[step, 0] = wx
        z_out[step, 1] = wy
        copies = [
            remote(z_out.at[step, 0], z_in.at[step, 0], z_sem.at[0, step, 0], z_sem.at[1, step, 0], place.down()),
            remote(z_out.at[step, 1], z_in.at[step, 1], z_sem.at[0, step, 1], z_sem.at[1, step, 1], place.right()),
        ]
        for copy in copies:
            copy.start()
        sent.extend(copies)
        own = jnp.concatenate([wx, wy], axis=1)
        acc[...] = jnp.dot(own, flex[0:HALF, :], preferred_element_type=F32)
        for copy in copies:
            copy.wait_recv()
        got = jnp.concatenate([-z_in[step, 0], -z_in[step, 1]], axis=1)
        acc[:, 0:HALF] += jnp.dot(got, flex[HALF:, 0:HALF], preferred_element_type=F32)
        copies = send_images(step + 1)
        acc[:, HALF:] += jnp.dot(got, flex[HALF:, HALF:], preferred_element_type=F32)
        return jumps(step + 1, copies)

    for copy in reads["low"]:
        copy.wait()
    acc[:, 0:HALF] = jnp.dot(loads[...], flex[:, 0:HALF], preferred_element_type=F32)
    wait_all_in()
    copies = send_images(0)
    for copy in reads["high"]:
        copy.wait()
    acc[:, HALF:] = jnp.dot(loads[...], flex[:, HALF:], preferred_element_type=F32)
    px, py = jumps(0, copies)
    vec[0, 0] = px
    vec[0, 1] = py
    qx, qy = operate(0, px, py)
    px, py = vec[0, 0], vec[0, 1]
    both = total(0, lanes(px * px + py * py, 0) + lanes(px * qx + py * qy, 64))
    rr = column(both, 0)
    step0 = rr / column(both, 64)
    rx = px - step0 * qx
    ry = py - step0 * qy
    vec[1, 0] = step0 * px
    vec[1, 1] = step0 * py
    s = column(total(1, lanes(rx * rx + ry * ry, 0)), 0)
    px = rx + (s / rr) * px
    py = ry + (s / rr) * py
    vec[0, 0] = px
    vec[0, 1] = py
    qx, qy = operate(1, px, py)
    px, py = vec[0, 0], vec[0, 1]
    step1 = s / column(total(2, lanes(px * qx + py * qy, 0)), 0)
    out_ref[...] = jnp.stack([vec[1, 0] + step1 * px, vec[1, 1] + step1 * py], axis=1).astype(BF16)
    for copy in sent + total.sent:
        copy.wait_send()


def start_reads(place, flex_hbm, loads_hbm, sizes_hbm, owner_hbm, flex, loads, meta, sem):
    reads = {
        "meta": [
            pltpu.make_async_copy(sizes_hbm.at[place.sy], meta.at[0], sem.at[0]),
            pltpu.make_async_copy(owner_hbm.at[place.sy], meta.at[1], sem.at[1]),
        ],
        "loads": [],
        "low": [],
        "high": [],
    }
    count = 2
    for at, block in enumerate(ROWS):
        reads["loads"].append(
            pltpu.make_async_copy(
                loads_hbm.at[0, 0, :, pl.ds(block * FACE, FACE)], loads.at[:, pl.ds(at * FACE, FACE)], sem.at[count]
            )
        )
        count += 1
    for col_at, col in enumerate(COLS):
        for at, block in enumerate(ROWS):
            reads["low" if col_at < 2 else "high"].append(
                pltpu.make_async_copy(
                    flex_hbm.at[0, 0, pl.ds(block * FACE, FACE), pl.ds(col * FACE, FACE)],
                    flex.at[pl.ds(at * FACE, FACE), pl.ds(col_at * FACE, FACE)],
                    sem.at[count],
                )
            )
            count += 1
    for group in ("loads", "low", "meta", "high"):
        for copy in reads[group]:
            copy.start()
    return reads


def coefficients(place, meta):
    lane = lax.broadcasted_iota(jnp.int32, (2, NSX), 1)
    here = lane == place.sx
    sizes = jnp.sum(jnp.where(here, meta[0].astype(F32), 0.0), axis=1, keepdims=True)
    owner = jnp.sum(jnp.where(here, meta[1].astype(F32), 0.0), axis=1, keepdims=True)
    spot = lax.broadcasted_iota(jnp.int32, (1, FACE), 1).astype(F32)
    sign = 1.0 - 2.0 * owner
    has_x = jnp.where(place.sx < NSX - 1, 1.0, 0.0).astype(F32)
    has_y = jnp.where(place.sy < NX - 1, 1.0, 0.0).astype(F32)
    cx = jnp.where(spot < sizes[0:1] * has_x, sign[0:1], 0.0)
    cy = jnp.where(spot < sizes[1:2] * has_y, sign[1:2], 0.0)
    return cx, cy


READS = 2 + 4 + 16


def exact(flexibility, loads, sizes, owner):
    return pl.pallas_call(
        exact_kernel,
        out_shape=jax.ShapeDtypeStruct((LOADS, 2, FACE), BF16),
        in_specs=[pl.BlockSpec(memory_space=pl.ANY)] * 4,
        out_specs=pl.BlockSpec(memory_space=pltpu.VMEM),
        scratch_shapes=[
            pltpu.VMEM((NB, NB), BF16),
            pltpu.VMEM((LOADS, NB), BF16),
            pltpu.VMEM((2, 2, NSX), jnp.int32),
            pltpu.VMEM((2, 2, LOADS, FACE), BF16),
            pltpu.VMEM((2, 2, LOADS, FACE), BF16),
            pltpu.VMEM((3, 2, LOADS, FACE), F32),
            pltpu.VMEM((3, 2, LOADS, FACE), F32),
            pltpu.VMEM((LOADS, NB), F32),
            pltpu.VMEM((2, 2, LOADS, FACE), F32),
        ]
        + [pltpu.VMEM((3, size, 1, 128), F32) for size in STAGES]
        + [
            pltpu.SemaphoreType.DMA((READS,)),
            pltpu.SemaphoreType.DMA((2, 2, 2)),
            pltpu.SemaphoreType.DMA((2, 3, 2)),
        ]
        + [pltpu.SemaphoreType.DMA((3, size)) for size in STAGES] * 2,
        compiler_params=pltpu.CompilerParams(collective_id=0, has_side_effects=True),
        name="exact",
    )(flexibility, loads, sizes, owner)


def far(size, k):
    return min(k, size - k)


PLANE = sorted(((x, y) for x in range(NX) for y in range(NY) if x or y), key=lambda o: -far(NX, o[0]) - far(NY, o[1]))
LINE = sorted(((z, c) for z in range(NZ) for c in range(2) if z or c), key=lambda o: -2 * far(NZ, o[0]) - o[1])


class Partners:
    def __init__(self, place):
        self.slots = (place.sy * NY + place.y, place.z * 2 + place.core)
        plane = [
            ((place.z * NY + lax.rem(place.y + y, NY)) * 2 + place.core, lax.rem(place.sy + x, NX)) for x, y in PLANE
        ]
        line = [
            (
                (lax.rem(place.z + z, NZ) * NY + place.y) * 2 + (1 - place.core if c else place.core),
                place.sy,
            )
            for z, c in LINE
        ]
        self.stages = (plane, line)
        self.core = (place.sx + 1 - 2 * place.core, place.sy)

    @staticmethod
    def along_y(place, k):
        return ((place.z * NY + lax.rem(place.y + k + NY, NY)) * 2 + place.core, place.sy)

    @staticmethod
    def along_z(place, k):
        return ((lax.rem(place.z + k + NZ, NZ) * NY + place.y) * 2 + place.core, place.sy)


def fast_kernel(
    flex_hbm, loads_hbm, sizes_hbm, owner_hbm, out_ref, good_ref,
    flex, loads, meta, sign_meta, u0, r0, u1, r1, dvec, qvec, low_ref,
    buf0, buf1,
    load_sem, u_sem, sum_sem, word,
):
    place = Place()
    left_sy = lax.rem(place.sy + NX - 1, NX)
    sem = iter(range(FAST_READS))
    load_read = pltpu.make_async_copy(loads_hbm.at[0, 0], loads, load_sem.at[next(sem)])
    flex_reads = {}
    for half in (1, 0):
        for block in range(4):
            spot = (pl.ds(block * FACE, FACE), pl.ds(half * HALF, HALF))
            flex_reads[half, block] = pltpu.make_async_copy(
                flex_hbm.at[(0, 0) + spot], flex.at[spot], load_sem.at[next(sem)]
            )
    meta_reads = [
        pltpu.make_async_copy(sizes_hbm.at[place.sy], meta.at[0], load_sem.at[next(sem)]),
        pltpu.make_async_copy(sizes_hbm.at[left_sy], meta.at[1], load_sem.at[next(sem)]),
        pltpu.make_async_copy(owner_hbm.at[place.sy], sign_meta, load_sem.at[next(sem)]),
    ]
    load_read.start()
    for half in (1, 0):
        for block in range(4):
            flex_reads[half, block].start()
    for copy in meta_reads:
        copy.start()
    partners = Partners(place)
    faces = (place.up(), place.down(), place.left(), place.right())
    near_y, near_z = [[along(place, k) for k in (1, -1)] for along in (partners.along_y, partners.along_z)]
    next_y, next_z = [[along(place, k) for k in (2, -2)] for along in (partners.along_y, partners.along_z)]
    rounds = (
        near_y + near_z,
        next_y + next_z,
        next_z + list(faces[2:]),
        [partners.core] + list(faces[2:]),
    )
    barrier = pltpu.get_barrier_semaphore()
    peers = list(faces) + near_y + near_z
    for peer in peers:
        pl.semaphore_signal(barrier, inc=1, device_id=peer, device_id_type=MESH)

    def tell(which):
        for peer in rounds[which]:
            pl.semaphore_signal(word.at[which], inc=1, device_id=peer, device_id_type=MESH)

    def hear(which):
        pl.semaphore_wait(word.at[which], len(rounds[which]))

    sent = []

    def exchange(step, half, source, into):
        copies = []
        for block in (2 * half, 2 * half + 1):
            copies.append(
                remote(
                    source.at[block], into.at[block ^ 1], u_sem.at[0, step, block], u_sem.at[1, step, block], faces[block]
                )
            )
            copies[-1].start()
        sent.extend(copies)
        return copies

    def product(rows, half, block):
        return jnp.dot(
            rows, flex[block * FACE : (block + 1) * FACE, half * HALF : (half + 1) * HALF], preferred_element_type=F32
        )

    def half_product(pair, row_half, col_half):
        return jnp.dot(
            pair,
            flex[row_half * HALF : (row_half + 1) * HALF, col_half * HALF : (col_half + 1) * HALF],
            preferred_element_type=F32,
        )

    load_read.wait()
    copies0 = {}
    for half in (1, 0):
        if half == 0:
            low_ref[0] = lax.dot_general(
                loads[:, HALF:], flex[0:HALF, HALF:], (((1,), (1,)), ((), ())), preferred_element_type=F32
            )
        for block in range(2):
            flex_reads[half, block].wait()
        value = half_product(loads[:, 0:HALF], 0, half)
        if half == 1:
            for block in range(2, 4):
                flex_reads[half, block].wait()
            value = value + half_product(loads[:, HALF:], 1, half)
        else:
            value = value + low_ref[0]
        u0[2 * half] = value[:, 0:FACE]
        u0[2 * half + 1] = value[:, FACE:]
        if half == 1:
            pl.semaphore_wait(barrier, len(peers))
        copies0[half] = exchange(0, half, u0, r0)
        if half == 1:
            tell(0)
    for copy in meta_reads:
        copy.wait()
    hear(0)
    tell(1)
    live, sign = live_faces(place, meta, sign_meta)
    hear(1)
    tell(2)

    def jump(half, copies, u, r, kept):
        for copy in copies[half]:
            copy.wait_recv()
        pair = []
        for block in (2 * half, 2 * half + 1):
            value = jnp.where(live[block], u[block] - r[block], 0.0)
            kept[block] = value
            pair.append(value.astype(BF16))
        return jnp.concatenate(pair, axis=1)

    pair = jump(0, copies0, u0, r0, dvec)
    for half in range(2):
        low_ref[half] = half_product(pair, 0, half)
    for block in range(2, 4):
        flex_reads[0, block].wait()
    pair = jump(1, copies0, u0, r0, dvec)
    copies1 = {}
    for half in (1, 0):
        value = low_ref[half] + half_product(pair, 1, half)
        u1[2 * half] = value[:, 0:FACE]
        u1[2 * half + 1] = value[:, FACE:]
        copies1[half] = exchange(1, half, u1, r1)
    hear(2)
    tell(3)
    top = lanes(dvec[1] * dvec[1] + dvec[3] * dvec[3], 0)
    first = jump(0, copies1, u1, r1, qvec)
    inner = first.astype(F32) * half_product(first, 0, 0)
    low_ref[0] = inner
    low_ref[1] = 2.0 * half_product(first, 0, 1)
    second = jump(1, copies1, u1, r1, qvec)
    inner = low_ref[0] + second.astype(F32) * (low_ref[1] + half_product(second, 1, 1))
    top = top + lanes(dvec[1] * qvec[1] + dvec[3] * qvec[3], 64)
    bottom = lanes(qvec[1] * qvec[1] + qvec[3] * qvec[3], 0) + lanes(inner, 64)
    sums = jnp.concatenate([top, bottom], axis=0)
    hear(3)
    waits = []
    for which, (stage, mine, buf) in enumerate(zip(partners.stages, partners.slots, (buf0, buf1))):
        buf[mine] = sums
        for peer in stage:
            remote(buf.at[mine], buf.at[mine], sum_sem.at[0, which], sum_sem.at[1, which], peer).start()
        others = buf.at[pl.ds(0, len(stage))]
        waits.append(remote(others, others, sum_sem.at[0, which], sum_sem.at[1, which], stage[0]))
        waits[-1].wait_recv()
        terms = [buf[k] for k in range(len(stage) + 1)]
        while len(terms) > 1:
            terms = [sum(terms[k : k + 2]) for k in range(0, len(terms), 2)]
        sums = terms[0]
    dd, dq = column(sums[0:1], 0), column(sums[0:1], 64)
    qq, qw = column(sums[1:2], 0), column(sums[1:2], 64)
    a = dd / dq
    far = a * a * qq
    s = far - dd
    g = far / dd
    weight = a * a * qw
    curve = g * g * dq - 2.0 * a * g * qq + weight
    a1 = s / curve
    alpha = a + a1 * g
    beta = -a1 * a
    mx = sign[0] * (alpha * dvec[1] + beta * qvec[1])
    my = sign[1] * (alpha * dvec[3] + beta * qvec[3])
    out_ref[...] = jnp.stack([mx, my], axis=1).astype(BF16)
    good = (s >= CLOSE * dd) & (curve >= CLOSE * weight) & (s < TOP) & (curve < TOP)
    for value in (dd, dq, qq, qw):
        good = good & (value > 1.0 / TOP) & (value < TOP)
    good_ref[0] = jnp.min(jnp.where(good, 1.0, 0.0)).astype(jnp.int32)
    for copy in sent + waits:
        copy.wait_send()


def live_faces(place, meta, sign_meta):
    lane = lax.broadcasted_iota(jnp.int32, (2, NSX), 1)

    def at(table, row):
        return jnp.sum(jnp.where(lane == row, table.astype(F32), 0.0), axis=1, keepdims=True)

    here = at(meta[0], place.sx)
    sizes = (
        at(meta[0], place.sx - 1)[0:1],
        here[0:1] * jnp.where(place.sx < NSX - 1, 1.0, 0.0).astype(F32),
        at(meta[1], place.sx)[1:2] * jnp.where(place.sy > 0, 1.0, 0.0).astype(F32),
        here[1:2] * jnp.where(place.sy < NX - 1, 1.0, 0.0).astype(F32),
    )
    spot = lax.broadcasted_iota(jnp.int32, (LOADS, FACE), 1).astype(F32)
    sign = 1.0 - 2.0 * at(sign_meta[...], place.sx)
    return [spot < size for size in sizes], (sign[0:1], sign[1:2])


FAST_READS = 1 + 8 + 3


CLOSE = 2.0**-6
TOP = 1e30


def fast(flexibility, loads, sizes, owner):
    def faces(dtype):
        return pltpu.VMEM((4, LOADS, FACE), dtype)

    return pl.pallas_call(
        fast_kernel,
        out_shape=(jax.ShapeDtypeStruct((LOADS, 2, FACE), BF16), jax.ShapeDtypeStruct((1,), jnp.int32)),
        in_specs=[pl.BlockSpec(memory_space=pl.ANY)] * 4,
        out_specs=(pl.BlockSpec(memory_space=pltpu.VMEM), pl.BlockSpec(memory_space=pltpu.SMEM)),
        scratch_shapes=[
            pltpu.VMEM((NB, NB), BF16),
            pltpu.VMEM((LOADS, NB), BF16),
            pltpu.VMEM((2, 2, NSX), jnp.int32),
            pltpu.VMEM((2, NSX), jnp.int32),
            faces(F32),
            faces(F32),
            faces(F32),
            faces(F32),
            faces(F32),
            faces(F32),
            pltpu.VMEM((2, LOADS, HALF), F32),
        ]
        + [pltpu.VMEM((size, 2, 128), F32) for size in (NX * NY, 2 * NZ)]
        + [
            pltpu.SemaphoreType.DMA((FAST_READS,)),
            pltpu.SemaphoreType.DMA((2, 2, 4)),
            pltpu.SemaphoreType.DMA((2, 2)),
            pltpu.SemaphoreType.REGULAR((4,)),
        ],
        compiler_params=pltpu.CompilerParams(collective_id=1, has_side_effects=True),
        name="fast",
    )(flexibility, loads, sizes, owner)


def body(flexibility, loads, face_sizes, face_owner):
    sizes = jnp.transpose(face_sizes, (1, 2, 0))
    owner = jnp.transpose(face_owner, (1, 2, 0))
    args = (flexibility, loads, sizes, owner)
    result, good = fast(*args)
    result = lax.cond(good[0] > 0, lambda: result, lambda: exact(*args))
    return jnp.transpose(result, (1, 0, 2))[None, None]

def solution(mesh):
    return jax.shard_map(
        body,
        mesh=mesh,
        in_specs=(P("sx", "sy", None, None), P("sx", "sy", None, None), P(), P()),
        out_specs=P("sx", "sy", None, None, None),
        check_vma=False,
    )
```

```python
import functools

import jax
import jax.numpy as jnp
from jax import lax
from jax.experimental import pallas as pl
from jax.experimental.pallas import tpu as pltpu
from jax.sharding import PartitionSpec as P

FACE = 384
NB = 4 * FACE
HALF = 2 * FACE
LOADS = 36
NX, NY, NZ = 4, 8, 12
NSX = NZ * NY * 2
MESH = pl.DeviceIdType.MESH
F32 = jnp.float32
BF16 = jnp.bfloat16
ROWS = (1, 3, 0, 2)
COLS = (0, 2, 1, 3)


class Place:
    def __init__(self):
        self.sx = lax.axis_index("sx")
        self.sy = lax.axis_index("sy")
        self.core = lax.rem(self.sx, 2)
        self.y = lax.rem(self.sx // 2, NY)
        self.z = self.sx // (2 * NY)
        self.near = self.sy * 2 + self.core

    def down(self):
        return (lax.rem(self.sx + 1, NSX), self.sy)

    def up(self):
        return (lax.rem(self.sx + NSX - 1, NSX), self.sy)

    def right(self):
        return (self.sx, lax.rem(self.sy + 1, NX))

    def left(self):
        return (self.sx, lax.rem(self.sy + NX - 1, NX))

    def stage(self, which, k):
        if which == 0:
            slot = lax.rem(self.near + k, 2 * NX)
            return (self.sx - self.core + lax.rem(slot, 2), slot // 2)
        if which == 1:
            y = lax.rem(self.y + k, NY)
            return ((self.z * NY + y) * 2 + self.core, self.sy)
        z = lax.rem(self.z + k, NZ)
        return ((z * NY + self.y) * 2 + self.core, self.sy)

    def slot(self, which):
        return (self.near, self.y, self.z)[which]


STAGES = (2 * NX, NY, NZ)


def greet(place):
    barrier = pltpu.get_barrier_semaphore()
    peers = [place.down(), place.up()]
    for which, size in enumerate(STAGES):
        peers += [place.stage(which, k) for k in range(1, size)]
    for peer in peers:
        pl.semaphore_signal(barrier, inc=1, device_id=peer, device_id_type=MESH)
    return functools.partial(pl.semaphore_wait, barrier, len(peers))


def remote(src, dst, send_sem, recv_sem, peer):
    return pltpu.make_async_remote_copy(
        src_ref=src, dst_ref=dst, send_sem=send_sem, recv_sem=recv_sem, device_id=peer, device_id_type=MESH
    )


def diagonal(offset):
    row = lax.broadcasted_iota(jnp.int32, (LOADS, 128), 0)
    lane = lax.broadcasted_iota(jnp.int32, (LOADS, 128), 1)
    return lane == row + offset


def lanes(product, offset):
    column = jnp.sum(product, axis=1, keepdims=True)
    return jnp.sum(jnp.where(diagonal(offset), column, 0.0), axis=0, keepdims=True)


def column(row, offset):
    return jnp.sum(jnp.where(diagonal(offset), row, 0.0), axis=1, keepdims=True)


class Sums:
    def __init__(self, place, bufs, send_sems, recv_sems):
        self.place, self.bufs, self.send_sems, self.recv_sems = place, bufs, send_sems, recv_sems
        self.sent = []

    def __call__(self, index, value):
        for which, size in enumerate(STAGES):
            buf = self.bufs[which].at[index]
            mine = self.place.slot(which)
            buf[mine] = value
            copies = []
            for k in range(1, size):
                copies.append(
                    remote(
                        buf.at[mine],
                        buf.at[mine],
                        self.send_sems[which].at[index, k],
                        self.recv_sems[which].at[index, k],
                        self.place.stage(which, k),
                    )
                )
                copies[-1].start()
            for copy in copies:
                copy.wait_recv()
            value = buf[0]
            for k in range(1, size):
                value = value + buf[k]
            self.sent += copies
        return value


def exact_kernel(
    flex_hbm, loads_hbm, sizes_hbm, owner_hbm, out_ref,
    flex, loads, meta, z_out, z_in, u_out, u_in, acc, vec,
    buf0, buf1, buf2,
    load_sem, z_sem, u_sem, send0, send1, send2, recv0, recv1, recv2,
):
    place = Place()
    wait_all_in = greet(place)
    reads = start_reads(place, flex_hbm, loads_hbm, sizes_hbm, owner_hbm, flex, loads, meta, load_sem)
    total = Sums(place, (buf0, buf1, buf2), (send0, send1, send2), (recv0, recv1, recv2))
    sent = []

    for copy in reads["meta"] + reads["loads"]:
        copy.wait()
    cx, cy = coefficients(place, meta)

    def send_images(step):
        u_out[step, 0] = acc[:, 0:FACE]
        u_out[step, 1] = acc[:, FACE:HALF]
        copies = [
            remote(u_out.at[step, 0], u_in.at[step, 0], u_sem.at[0, step, 0], u_sem.at[1, step, 0], place.up()),
            remote(u_out.at[step, 1], u_in.at[step, 1], u_sem.at[0, step, 1], u_sem.at[1, step, 1], place.left()),
        ]
        for copy in copies:
            copy.start()
        sent.extend(copies)
        return copies

    def jumps(step, copies):
        for copy in copies:
            copy.wait_recv()
        jx = cx * (acc[:, HALF : HALF + FACE] - u_in[step, 0])
        jy = cy * (acc[:, HALF + FACE :] - u_in[step, 1])
        return jx, jy

    def operate(step, px, py):
        wx = (cx * px).astype(BF16)
        wy = (cy * py).astype(BF16)
        z_out[step, 0] = wx
        z_out[step, 1] = wy
        copies = [
            remote(z_out.at[step, 0], z_in.at[step, 0], z_sem.at[0, step, 0], z_sem.at[1, step, 0], place.down()),
            remote(z_out.at[step, 1], z_in.at[step, 1], z_sem.at[0, step, 1], z_sem.at[1, step, 1], place.right()),
        ]
        for copy in copies:
            copy.start()
        sent.extend(copies)
        own = jnp.concatenate([wx, wy], axis=1)
        acc[...] = jnp.dot(own, flex[0:HALF, :], preferred_element_type=F32)
        for copy in copies:
            copy.wait_recv()
        got = jnp.concatenate([-z_in[step, 0], -z_in[step, 1]], axis=1)
        acc[:, 0:HALF] += jnp.dot(got, flex[HALF:, 0:HALF], preferred_element_type=F32)
        copies = send_images(step + 1)
        acc[:, HALF:] += jnp.dot(got, flex[HALF:, HALF:], preferred_element_type=F32)
        return jumps(step + 1, copies)

    for copy in reads["low"]:
        copy.wait()
    acc[:, 0:HALF] = jnp.dot(loads[...], flex[:, 0:HALF], preferred_element_type=F32)
    wait_all_in()
    copies = send_images(0)
    for copy in reads["high"]:
        copy.wait()
    acc[:, HALF:] = jnp.dot(loads[...], flex[:, HALF:], preferred_element_type=F32)
    px, py = jumps(0, copies)
    vec[0, 0] = px
    vec[0, 1] = py
    qx, qy = operate(0, px, py)
    px, py = vec[0, 0], vec[0, 1]
    both = total(0, lanes(px * px + py * py, 0) + lanes(px * qx + py * qy, 64))
    rr = column(both, 0)
    step0 = rr / column(both, 64)
    rx = px - step0 * qx
    ry = py - step0 * qy
    vec[1, 0] = step0 * px
    vec[1, 1] = step0 * py
    s = column(total(1, lanes(rx * rx + ry * ry, 0)), 0)
    px = rx + (s / rr) * px
    py = ry + (s / rr) * py
    vec[0, 0] = px
    vec[0, 1] = py
    qx, qy = operate(1, px, py)
    px, py = vec[0, 0], vec[0, 1]
    step1 = s / column(total(2, lanes(px * qx + py * qy, 0)), 0)
    out_ref[0] = (vec[1, 0] + step1 * px).astype(BF16)
    out_ref[1] = (vec[1, 1] + step1 * py).astype(BF16)
    for copy in sent + total.sent:
        copy.wait_send()


def start_reads(place, flex_hbm, loads_hbm, sizes_hbm, owner_hbm, flex, loads, meta, sem):
    reads = {
        "meta": [
            pltpu.make_async_copy(sizes_hbm.at[place.sy], meta.at[0], sem.at[0]),
            pltpu.make_async_copy(owner_hbm.at[place.sy], meta.at[1], sem.at[1]),
        ],
        "loads": [],
        "low": [],
        "high": [],
    }
    count = 2
    for at, block in enumerate(ROWS):
        reads["loads"].append(
            pltpu.make_async_copy(
                loads_hbm.at[0, 0, :, pl.ds(block * FACE, FACE)], loads.at[:, pl.ds(at * FACE, FACE)], sem.at[count]
            )
        )
        count += 1
    for col_at, col in enumerate(COLS):
        for at, block in enumerate(ROWS):
            reads["low" if col_at < 2 else "high"].append(
                pltpu.make_async_copy(
                    flex_hbm.at[0, 0, pl.ds(block * FACE, FACE), pl.ds(col * FACE, FACE)],
                    flex.at[pl.ds(at * FACE, FACE), pl.ds(col_at * FACE, FACE)],
                    sem.at[count],
                )
            )
            count += 1
    for group in ("loads", "low", "meta", "high"):
        for copy in reads[group]:
            copy.start()
    return reads


def coefficients(place, meta):
    lane = lax.broadcasted_iota(jnp.int32, (2, NSX), 1)
    here = lane == place.sx
    sizes = jnp.sum(jnp.where(here, meta[0].astype(F32), 0.0), axis=1, keepdims=True)
    owner = jnp.sum(jnp.where(here, meta[1].astype(F32), 0.0), axis=1, keepdims=True)
    spot = lax.broadcasted_iota(jnp.int32, (1, FACE), 1).astype(F32)
    sign = 1.0 - 2.0 * owner
    has_x = jnp.where(place.sx < NSX - 1, 1.0, 0.0).astype(F32)
    has_y = jnp.where(place.sy < NX - 1, 1.0, 0.0).astype(F32)
    cx = jnp.where(spot < sizes[0:1] * has_x, sign[0:1], 0.0)
    cy = jnp.where(spot < sizes[1:2] * has_y, sign[1:2], 0.0)
    return cx, cy


READS = 2 + 4 + 16


def exact(flexibility, loads, sizes, owner):
    return pl.pallas_call(
        exact_kernel,
        out_shape=jax.ShapeDtypeStruct((2, LOADS, FACE), BF16),
        in_specs=[pl.BlockSpec(memory_space=pl.ANY)] * 4,
        out_specs=pl.BlockSpec(memory_space=pltpu.VMEM),
        scratch_shapes=[
            pltpu.VMEM((NB, NB), BF16),
            pltpu.VMEM((LOADS, NB), BF16),
            pltpu.VMEM((2, 2, NSX), jnp.int32),
            pltpu.VMEM((2, 2, LOADS, FACE), BF16),
            pltpu.VMEM((2, 2, LOADS, FACE), BF16),
            pltpu.VMEM((3, 2, LOADS, FACE), F32),
            pltpu.VMEM((3, 2, LOADS, FACE), F32),
            pltpu.VMEM((LOADS, NB), F32),
            pltpu.VMEM((2, 2, LOADS, FACE), F32),
        ]
        + [pltpu.VMEM((3, size, 1, 128), F32) for size in STAGES]
        + [
            pltpu.SemaphoreType.DMA((READS,)),
            pltpu.SemaphoreType.DMA((2, 2, 2)),
            pltpu.SemaphoreType.DMA((2, 3, 2)),
        ]
        + [pltpu.SemaphoreType.DMA((3, size)) for size in STAGES] * 2,
        compiler_params=pltpu.CompilerParams(collective_id=0, has_side_effects=True),
        name="exact",
    )(flexibility, loads, sizes, owner)


def far(size, k):
    return min(k, size - k)


PLANE = sorted(((x, y) for x in range(NX) for y in range(NY) if x or y), key=lambda o: -far(NX, o[0]) - far(NY, o[1]))
LINE = sorted(((z, c) for z in range(NZ) for c in range(2) if z or c), key=lambda o: -2 * far(NZ, o[0]) - o[1])


class Partners:
    def __init__(self, place):
        self.slots = (place.sy * NY + place.y, place.z * 2 + place.core)
        plane = [
            ((place.z * NY + lax.rem(place.y + y, NY)) * 2 + place.core, lax.rem(place.sy + x, NX)) for x, y in PLANE
        ]
        line = [
            (
                (lax.rem(place.z + z, NZ) * NY + place.y) * 2 + (1 - place.core if c else place.core),
                place.sy,
            )
            for z, c in LINE
        ]
        self.stages = (plane, line)
        self.core = (place.sx + 1 - 2 * place.core, place.sy)

    @staticmethod
    def along_y(place, k):
        return ((place.z * NY + lax.rem(place.y + k + NY, NY)) * 2 + place.core, place.sy)

    @staticmethod
    def along_z(place, k):
        return ((lax.rem(place.z + k + NZ, NZ) * NY + place.y) * 2 + place.core, place.sy)


def fast_kernel(
    flex_hbm, loads_hbm, sizes_hbm, owner_hbm, out_ref, good_ref,
    flex, loads, meta, sign_meta, u0, r0, u1, r1, dvec, qvec, low_ref,
    buf0, buf1,
    load_sem, u_sem, sum_sem, word,
):
    place = Place()
    left_sy = lax.rem(place.sy + NX - 1, NX)
    sem = iter(range(FAST_READS))
    load_read = pltpu.make_async_copy(loads_hbm.at[0, 0], loads, load_sem.at[next(sem)])
    flex_reads = {}
    for half in (1, 0):
        for block in range(4):
            spot = (pl.ds(block * FACE, FACE), pl.ds(half * HALF, HALF))
            flex_reads[half, block] = pltpu.make_async_copy(
                flex_hbm.at[(0, 0) + spot], flex.at[spot], load_sem.at[next(sem)]
            )
    meta_reads = [
        pltpu.make_async_copy(sizes_hbm.at[place.sy], meta.at[0], load_sem.at[next(sem)]),
        pltpu.make_async_copy(sizes_hbm.at[left_sy], meta.at[1], load_sem.at[next(sem)]),
        pltpu.make_async_copy(owner_hbm.at[place.sy], sign_meta, load_sem.at[next(sem)]),
    ]
    load_read.start()
    for half in (1, 0):
        for block in range(4):
            flex_reads[half, block].start()
    for copy in meta_reads:
        copy.start()
    partners = Partners(place)
    faces = (place.up(), place.down(), place.left(), place.right())
    near_y, near_z = [[along(place, k) for k in (1, -1)] for along in (partners.along_y, partners.along_z)]
    next_y, next_z = [[along(place, k) for k in (2, -2)] for along in (partners.along_y, partners.along_z)]
    rounds = (
        near_y + near_z,
        next_y + next_z,
        next_z + list(faces[2:]),
        [partners.core] + list(faces[2:]),
    )
    barrier = pltpu.get_barrier_semaphore()
    peers = list(faces) + near_y + near_z
    for peer in peers:
        pl.semaphore_signal(barrier, inc=1, device_id=peer, device_id_type=MESH)

    def tell(which):
        for peer in rounds[which]:
            pl.semaphore_signal(word.at[which], inc=1, device_id=peer, device_id_type=MESH)

    def hear(which):
        pl.semaphore_wait(word.at[which], len(rounds[which]))

    sent = []

    def exchange(step, half, source, into):
        copies = []
        for block in (2 * half, 2 * half + 1):
            copies.append(
                remote(
                    source.at[block], into.at[block ^ 1], u_sem.at[0, step, block], u_sem.at[1, step, block], faces[block]
                )
            )
            copies[-1].start()
        sent.extend(copies)
        return copies

    def product(rows, half, block):
        return jnp.dot(
            rows, flex[block * FACE : (block + 1) * FACE, half * HALF : (half + 1) * HALF], preferred_element_type=F32
        )

    def half_product(pair, row_half, col_half):
        return jnp.dot(
            pair,
            flex[row_half * HALF : (row_half + 1) * HALF, col_half * HALF : (col_half + 1) * HALF],
            preferred_element_type=F32,
        )

    load_read.wait()
    copies0 = {}
    for half in (1, 0):
        for block in range(2):
            flex_reads[half, block].wait()
        value = half_product(loads[:, 0:HALF], 0, half)
        for block in range(2, 4):
            flex_reads[half, block].wait()
        value = value + half_product(loads[:, HALF:], 1, half)
        u0[2 * half] = value[:, 0:FACE]
        u0[2 * half + 1] = value[:, FACE:]
        if half == 1:
            pl.semaphore_wait(barrier, len(peers))
        copies0[half] = exchange(0, half, u0, r0)
        if half == 1:
            tell(0)
    for copy in meta_reads:
        copy.wait()
    hear(0)
    tell(1)
    live, sign = live_faces(place, meta, sign_meta)
    hear(1)
    tell(2)

    def jump(half, copies, u, r, kept):
        for copy in copies[half]:
            copy.wait_recv()
        pair = []
        for block in (2 * half, 2 * half + 1):
            value = jnp.where(live[block], u[block] - r[block], 0.0)
            kept[block] = value
            pair.append(value.astype(BF16))
        return jnp.concatenate(pair, axis=1)

    pair = jump(0, copies0, u0, r0, dvec)
    for half in range(2):
        low_ref[half] = half_product(pair, 0, half)
    pair = jump(1, copies0, u0, r0, dvec)
    copies1 = {}
    for half in (1, 0):
        value = low_ref[half] + half_product(pair, 1, half)
        u1[2 * half] = value[:, 0:FACE]
        u1[2 * half + 1] = value[:, FACE:]
        copies1[half] = exchange(1, half, u1, r1)
    hear(2)
    tell(3)
    top = lanes(dvec[1] * dvec[1] + dvec[3] * dvec[3], 0)
    first = jump(0, copies1, u1, r1, qvec)
    low_ref[0] = first.astype(F32) * half_product(first, 0, 0)
    low_ref[1] = 2.0 * half_product(first, 0, 1)
    second = jump(1, copies1, u1, r1, qvec)
    inner = low_ref[0] + second.astype(F32) * (low_ref[1] + half_product(second, 1, 1))
    top = top + lanes(dvec[1] * qvec[1] + dvec[3] * qvec[3], 64)
    bottom = lanes(qvec[1] * qvec[1] + qvec[3] * qvec[3], 0) + lanes(inner, 64)
    sums = jnp.concatenate([top, bottom], axis=0)
    hear(3)
    waits = []
    for which, (stage, mine, buf) in enumerate(zip(partners.stages, partners.slots, (buf0, buf1))):
        buf[mine] = sums
        for peer in stage:
            remote(buf.at[mine], buf.at[mine], sum_sem.at[0, which], sum_sem.at[1, which], peer).start()
        others = buf.at[pl.ds(0, len(stage))]
        waits.append(remote(others, others, sum_sem.at[0, which], sum_sem.at[1, which], stage[0]))
        waits[-1].wait_recv()
        terms = [buf[k] for k in range(len(stage) + 1)]
        while len(terms) > 1:
            terms = [sum(terms[k : k + 2]) for k in range(0, len(terms), 2)]
        sums = terms[0]
    dd, dq = column(sums[0:1], 0), column(sums[0:1], 64)
    qq, qw = column(sums[1:2], 0), column(sums[1:2], 64)
    a = dd / dq
    far = a * a * qq
    s = far - dd
    g = far / dd
    weight = a * a * qw
    curve = g * g * dq - 2.0 * a * g * qq + weight
    a1 = s / curve
    alpha = a + a1 * g
    beta = -a1 * a
    out_ref[0] = (sign[0] * (alpha * dvec[1] + beta * qvec[1])).astype(BF16)
    out_ref[1] = (sign[1] * (alpha * dvec[3] + beta * qvec[3])).astype(BF16)
    good = (s >= CLOSE * dd) & (curve >= CLOSE * weight) & (s < TOP) & (curve < TOP)
    for value in (dd, dq, qq, qw):
        good = good & (value > 1.0 / TOP) & (value < TOP)
    good_ref[0] = jnp.min(jnp.where(good, 1.0, 0.0)).astype(jnp.int32)
    for copy in sent + waits:
        copy.wait_send()


def live_faces(place, meta, sign_meta):
    lane = lax.broadcasted_iota(jnp.int32, (2, NSX), 1)

    def at(table, row):
        return jnp.sum(jnp.where(lane == row, table.astype(F32), 0.0), axis=1, keepdims=True)

    here = at(meta[0], place.sx)
    sizes = (
        at(meta[0], place.sx - 1)[0:1],
        here[0:1] * jnp.where(place.sx < NSX - 1, 1.0, 0.0).astype(F32),
        at(meta[1], place.sx)[1:2] * jnp.where(place.sy > 0, 1.0, 0.0).astype(F32),
        here[1:2] * jnp.where(place.sy < NX - 1, 1.0, 0.0).astype(F32),
    )
    spot = lax.broadcasted_iota(jnp.int32, (LOADS, FACE), 1).astype(F32)
    sign = 1.0 - 2.0 * at(sign_meta[...], place.sx)
    return [spot < size for size in sizes], (sign[0:1], sign[1:2])


FAST_READS = 1 + 8 + 3


CLOSE = 2.0**-6
TOP = 1e30


def fast(flexibility, loads, sizes, owner):
    def faces(dtype):
        return pltpu.VMEM((4, LOADS, FACE), dtype)

    return pl.pallas_call(
        fast_kernel,
        out_shape=(jax.ShapeDtypeStruct((2, LOADS, FACE), BF16), jax.ShapeDtypeStruct((1,), jnp.int32)),
        in_specs=[pl.BlockSpec(memory_space=pl.ANY)] * 4,
        out_specs=(pl.BlockSpec(memory_space=pltpu.VMEM), pl.BlockSpec(memory_space=pltpu.SMEM)),
        scratch_shapes=[
            pltpu.VMEM((NB, NB), BF16),
            pltpu.VMEM((LOADS, NB), BF16),
            pltpu.VMEM((2, 2, NSX), jnp.int32),
            pltpu.VMEM((2, NSX), jnp.int32),
            faces(F32),
            faces(F32),
            faces(F32),
            faces(F32),
            faces(F32),
            faces(F32),
            pltpu.VMEM((2, LOADS, HALF), F32),
        ]
        + [pltpu.VMEM((size, 2, 128), F32) for size in (NX * NY, 2 * NZ)]
        + [
            pltpu.SemaphoreType.DMA((FAST_READS,)),
            pltpu.SemaphoreType.DMA((2, 2, 4)),
            pltpu.SemaphoreType.DMA((2, 2)),
            pltpu.SemaphoreType.REGULAR((4,)),
        ],
        compiler_params=pltpu.CompilerParams(collective_id=1, has_side_effects=True),
        name="fast",
    )(flexibility, loads, sizes, owner)


def body(flexibility, loads, face_sizes, face_owner):
    sizes = jnp.transpose(face_sizes, (1, 2, 0))
    owner = jnp.transpose(face_owner, (1, 2, 0))
    args = (flexibility, loads, sizes, owner)
    result, good = fast(*args)
    result = lax.cond(good[0] > 0, lambda: result, lambda: exact(*args))
    return result[None, None]

def solution(mesh):
    return jax.shard_map(
        body,
        mesh=mesh,
        in_specs=(P("sx", "sy", None, None), P("sx", "sy", None, None), P(), P()),
        out_specs=P("sx", "sy", None, None, None),
        check_vma=False,
    )
```
